128 devices in a mesh: rows: 16 (over z, y), zone: 8 (over x, core).
Axes of the slice: x: 4, y: 4, z: 4, core: 2. Of those that a mesh axis runs over, the one named last changes fastest.
Arguments:
- snapshots: float32 [1048576, 256], P(('rows', 'zone')), may hold values from -6 to 6
- tangent: bfloat16 [1048576, 512], P(('rows', 'zone')), may hold values from -0.25 to 0.25
- pattern: int32 [8192, 4], P(('rows', 'zone')), may hold values from 0 to 259, as said below
- forcing: float32 [1048576], P(('rows', 'zone')), may hold values from -6 to 6
- step_index: int32 [256], replicated, may hold values from 0 to 255, each once
Outputs:
- basis: float32 [1048576, 256], P(('rows', 'zone'))
- coefficients: float32 [3, 256], replicated
- residual: float32 [1048576], P(('rows', 'zone'))
The draws below stay inside these ranges and needn't reach their ends.
Inputs may be any that keep to these rules, and one draw needn't show every extreme that they name: `pattern`: codes of sources 1 and 3 name one of the last 4 blocks of the neighbour, codes of sources 2 and 4 one of its first 4 blocks. `step_index`: each step index once.
All inputs are finite; a program needn't handle non-finite values.
Results may differ from the reference program's by a relative error of at most 0.0003.
Values sent between devices are 32-bit elements; how exact they have to be, the bound alone decides.
A program may use at most 320 MiB of HBM per device.

```python
import math
import jax
import jax.numpy as jnp
from jax import lax

SNAPS = 256
ROWS_DEV = 8192
BLOCK = 128
COUPLED = 4
HALO = 4
STEPS = 3
BLK_DEV = 64
NDOF = 1048576
N_ROWS = 16
N_ZONE = 8


smooth_waves = 4


def draw_snapshots(key, part):
    key_noise, key_amplitude = jax.random.split(jax.random.fold_in(key, 101))
    position = jnp.arange(NDOF, dtype=jnp.float32) / NDOF
    noise_part = jax.random.normal(key_noise, (NDOF, SNAPS), jnp.float32)
    amplitude = jax.random.normal(key_amplitude, (2 * smooth_waves, SNAPS), jnp.float32) * 0.6
    summed = noise_part
    for wave_index in range(smooth_waves):
        wave_phase = 2.0 * math.pi * (wave_index + 1) * position
        summed = summed + jnp.cos(wave_phase)[:, None] * amplitude[2 * wave_index][None, :]
        summed = summed + jnp.sin(wave_phase)[:, None] * amplitude[2 * wave_index + 1][None, :]
    return jnp.clip(summed, -6.0, 6.0)


def draw_tangent(key, part):
    key_noise, key_level = jax.random.split(jax.random.fold_in(key, 202))
    tile_width = COUPLED * BLOCK
    noise_scale = float(tile_width) ** (-0.5)
    noise_part = jax.random.normal(key_noise, (NDOF, tile_width), jnp.float32) * noise_scale
    coherent_level = jax.random.uniform(key_level, (NDOF // BLOCK, COUPLED), jnp.float32, 0.5, 1.5) / tile_width
    coherent_part = jnp.repeat(jnp.repeat(coherent_level, BLOCK, axis=0), BLOCK, axis=1)
    return jnp.clip(noise_part + coherent_part, -0.25, 0.25).astype(jnp.bfloat16)


def draw_pattern(key, part):
    key_source, key_local, key_edge = jax.random.split(key, 3)
    shape = (NDOF // BLOCK, COUPLED)
    picker = jax.random.randint(key_source, shape, 0, 8)
    source = jnp.maximum(picker - 3, 0)
    local_block = jax.random.randint(key_local, shape, 0, BLK_DEV)
    edge_block = jax.random.randint(key_edge, shape, 0, HALO)
    from_tail = (source == 1) | (source == 3)
    block_pick = jnp.where(source == 0, local_block, jnp.where(from_tail, BLK_DEV - HALO + edge_block, edge_block))
    codes = source * BLK_DEV + block_pick
    codes = codes.at[0, 0].set(4 * BLK_DEV + HALO - 1)
    codes = codes.at[1, 0].set(0)
    return codes.astype(jnp.int32)


def shard_levels(stream_key, shape, cuts, smallest, largest):
    loudness = 1.0
    for dim, blocks in cuts:
        heights = jax.random.uniform(jax.random.fold_in(jax.random.fold_in(stream_key, 6), dim), (blocks,), jnp.float32, smallest / len(cuts), largest / len(cuts))
        loudness = loudness * jnp.repeat(jnp.exp(heights), shape[dim] // blocks).reshape((-1,) + (1,) * (len(shape) - 1 - dim))
    return loudness


def gaussian(rng, dims, width, most, pieces=(), held_as=jnp.bfloat16):
    drawn = width * jax.random.normal(rng, dims, jnp.float32)
    if pieces:
        drawn = drawn * shard_levels(rng, dims, pieces, -0.22, 0.18)
    return jnp.clip(drawn, -most, most).astype(held_as)


def setup_inputs(seed: int = 0) -> dict:
    arg_keys = jax.random.split(jax.random.key(seed), 6)
    snapshots = draw_snapshots(jax.random.fold_in(arg_keys[5], 71), 0)
    tangent = draw_tangent(jax.random.fold_in(arg_keys[5], 71), 0)
    pattern = draw_pattern(jax.random.fold_in(arg_keys[5], 71), 0)
    forcing = gaussian(arg_keys[3], (NDOF,), 1.0, 6.0, ((0, 128),), jnp.float32)
    step_index = jax.random.permutation(arg_keys[4], SNAPS).astype(jnp.int32)
    return dict(snapshots=snapshots, tangent=tangent, pattern=pattern, forcing=forcing, step_index=step_index)


step_size = 0.25

def tangent_product(field_in, tangent, pattern):
    highest = lax.Precision.HIGHEST
    block_count = NDOF // BLOCK
    device_count = NDOF // ROWS_DEV
    block_index = jnp.arange(block_count, dtype=jnp.int32)
    device_of = (block_index // BLK_DEV)[:, None]
    row_of = device_of // N_ZONE
    zone_of = device_of % N_ZONE
    source = pattern // BLK_DEV
    block_pick = pattern % BLK_DEV
    target_row = jnp.where(source == 1, (row_of - 1) % N_ROWS, jnp.where(source == 2, (row_of + 1) % N_ROWS, row_of))
    target_zone = jnp.where(source == 3, zone_of - 1, jnp.where(source == 4, zone_of + 1, zone_of))
    present = (target_zone >= 0) & (target_zone < N_ZONE)
    col_block = ((target_row * N_ZONE + jnp.clip(target_zone, 0, N_ZONE - 1)) * BLK_DEV + block_pick).astype(jnp.int32)
    blocks = field_in.reshape(block_count, BLOCK, SNAPS)
    tile_blocks = tangent.reshape(device_count, BLK_DEV, BLOCK, COUPLED, BLOCK)
    col_block = col_block.reshape(device_count, BLK_DEV, COUPLED)
    present = present.reshape(device_count, BLK_DEV, COUPLED)

    def one_device(item):
        tiles, columns, mask_here = item
        picked = blocks[columns] * mask_here.astype(jnp.float32)[:, :, None, None]
        return jnp.einsum('gbec,gecs->gbs', tiles.astype(jnp.float32), picked, precision=highest)
    product = lax.map(one_device, (tile_blocks, col_block, present))
    return product.reshape(NDOF, SNAPS)

def reference(snapshots, tangent, pattern, forcing, step_index):
    highest = lax.Precision.HIGHEST
    inverse_count = 1.0 / NDOF
    identity = jnp.eye(SNAPS, dtype=jnp.float32)
    gram_matrix = jnp.dot(snapshots.T, snapshots, precision=highest) * inverse_count
    factor_low = jnp.linalg.cholesky(gram_matrix)
    inverse = jax.scipy.linalg.solve_triangular(factor_low, identity, lower=True).T
    basis = jnp.dot(snapshots, inverse, precision=highest)
    tangent_image = tangent_product(basis, tangent, pattern)
    trial_basis = basis + step_size * tangent_image
    normal = jnp.dot(trial_basis.T, trial_basis, precision=highest) * inverse_count
    project = jnp.dot(trial_basis.T, basis, precision=highest) * inverse_count
    load_vector = jnp.dot(trial_basis.T, forcing, precision=highest) * inverse_count
    latest = (step_index == jnp.max(step_index)).astype(jnp.float32)
    coeff_now = jnp.dot(latest, factor_low, precision=highest)
    normal_low = jnp.linalg.cholesky(normal)
    history = []
    coeff_old = coeff_now
    for iteration in range(STEPS):
        coeff_old = coeff_now
        right_side = jnp.dot(project, coeff_now, precision=highest) + step_size * load_vector
        coeff_now = jax.scipy.linalg.cho_solve((normal_low, True), right_side)
        history.append(coeff_now)
    residual = jnp.dot(trial_basis, coeff_now, precision=highest) - jnp.dot(basis, coeff_old, precision=highest) - step_size * forcing
    return (basis, jnp.stack(history), residual)
```

```python
import functools

import jax
import jax.numpy as jnp
from jax import lax
from jax.experimental import pallas as pl
from jax.experimental.pallas import tpu as pltpu
from jax.sharding import PartitionSpec as P

HALO = 4
STEPS = 3
STEP = 0.25
B = 128
N = 256
CHUNK = 1024
PACK = 1536
F32 = jnp.float32
BF16 = jnp.bfloat16
HI = lax.Precision.HIGHEST
MESH = pl.DeviceIdType.MESH


def split(x):
    hi = x.astype(BF16)
    return hi, (x - hi.astype(F32)).astype(BF16)


def tdot(a, b):
    return lax.dot_general(a, b, (((0,), (0,)), ((), ())), preferred_element_type=F32)


def gram_kernel(s_ref, sh_ref, sl_ref, g_ref):
    step = pl.program_id(0)

    @pl.when(step == 0)
    def _():
        g_ref[...] = jnp.zeros_like(g_ref)

    hi, lo = split(s_ref[...])
    sh_ref[...] = hi
    sl_ref[...] = lo
    g_ref[...] += tdot(hi, hi)


def gram(snapshots):
    rows = snapshots.shape[0]
    return pl.pallas_call(
        gram_kernel,
        grid=(rows // CHUNK,),
        in_specs=[pl.BlockSpec((CHUNK, N), lambda i: (i, 0))],
        out_specs=[
            pl.BlockSpec((CHUNK, N), lambda i: (i, 0)),
            pl.BlockSpec((CHUNK, N), lambda i: (i, 0)),
            pl.BlockSpec((N, N), lambda i: (0, 0)),
        ],
        out_shape=[
            jax.ShapeDtypeStruct((rows, N), BF16),
            jax.ShapeDtypeStruct((rows, N), BF16),
            jax.ShapeDtypeStruct((N, N), F32),
        ],
        compiler_params=pltpu.CompilerParams(vmem_limit_bytes=24 << 20),
        cost_estimate=pl.CostEstimate(flops=4 * rows * N * N, bytes_accessed=8 * rows * N, transcendentals=0),
        name="gram",
    )(snapshots)


def image_kernel(
    index_ref, t_ref, f_ref, g_ref, rp_ref, rn_ref, zp_ref, zn_ref, sh_hbm, sl_hbm, y_ref, pack_ref,
    cand_h, cand_l, left, right, acc, load_acc, sem,
):
    step = pl.program_id(0)
    rows = sh_hbm.shape[0]
    edge = HALO * B

    @pl.when(step == 0)
    def _():
        one = pltpu.make_async_copy(sh_hbm, cand_h.at[pl.ds(0, rows)], sem.at[0])
        two = pltpu.make_async_copy(sl_hbm, cand_l.at[pl.ds(0, rows)], sem.at[1])
        one.start()
        two.start()
        for i, ref in enumerate((rp_ref, rn_ref, zp_ref, zn_ref)):
            hi, lo = split(ref[...])
            cand_h[pl.ds(rows + i * edge, edge), :] = hi
            cand_l[pl.ds(rows + i * edge, edge), :] = lo
        acc[...] = jnp.zeros_like(acc)
        load_acc[...] = jnp.zeros_like(load_acc)
        one.wait()
        two.wait()

    groups = CHUNK // B
    force = f_ref[...].T
    total = jnp.zeros((8, N), F32)
    for g in range(groups):
        picks = [pl.ds(pl.multiple_of(index_ref[step * groups + g, e] * B, B), B) for e in range(4)]
        tiles = t_ref[g * B : (g + 1) * B, :]
        image = jnp.dot(tiles, jnp.concatenate([cand_h[p, :] for p in picks], axis=0), preferred_element_type=F32)
        image += jnp.dot(tiles, jnp.concatenate([cand_l[p, :] for p in picks], axis=0), preferred_element_type=F32)
        own = pl.ds(pl.multiple_of(step * CHUNK + g * B, B), B)
        y = cand_h[own, :].astype(F32) + cand_l[own, :].astype(F32) + STEP * image
        y_ref[g * B : (g + 1) * B, :] = y
        hi, lo = split(y)
        left[g * B : (g + 1) * B, :N] = hi
        left[g * B : (g + 1) * B, N : 2 * N] = lo
        right[g * B : (g + 1) * B, N:] = hi
        total += jnp.sum((y * force[:, g : g + 1]).reshape(B // 8, 8, N), axis=0)
    load_acc[...] += total
    here = pl.ds(pl.multiple_of(step * CHUNK, CHUNK), CHUNK)
    left[:, 2 * N :] = cand_l[here, :]
    right[:, :N] = cand_h[here, :]
    both = tdot(left[...], right[...])
    acc[0] += both[:N, :N] + both[N : 2 * N, :N]
    acc[1] += both[:N, N:] * 0.5 + both[N : 2 * N, N:]
    acc[2] += both[2 * N :, N:]
    acc[3] += both[2 * N :, :N]

    @pl.when(step == pl.num_programs(0) - 1)
    def _():
        normal = acc[1] + acc[1].T
        project = acc[0] + acc[2].T
        half = g_ref[...] * 0.5 + acc[3]
        gram_matrix = half + half.T
        blocks = []
        for matrix in (gram_matrix, normal):
            blocks += [matrix[:B, :B], matrix[:B, B:], matrix[B:, B:]]
        blocks += [project[:B, :B], project[:B, B:], project[B:, :B], project[B:, B:]]
        for i, block in enumerate(blocks):
            pack_ref[i * B : (i + 1) * B, :] = block
        load = jnp.sum(load_acc[...], axis=0, keepdims=True)
        pack_ref[10 * B :, :] = jnp.zeros((PACK - 10 * B, B), F32)
        pack_ref[10 * B : 10 * B + 1, :] = load[:, :B]
        pack_ref[10 * B + 1 : 10 * B + 2, :] = load[:, B:]


def image(index_map, tangent, forcing, gram_local, halos, sh, sl):
    rows = sh.shape[0]
    edge = HALO * B
    whole = lambda i, *_: (0, 0)
    return pl.pallas_call(
        image_kernel,
        grid_spec=pltpu.PrefetchScalarGridSpec(
            num_scalar_prefetch=1,
            grid=(rows // CHUNK,),
            in_specs=[
                pl.BlockSpec((CHUNK, 4 * B), lambda i, *_: (i, 0)),
                pl.BlockSpec((CHUNK // B, B), lambda i, *_: (i, 0)),
                pl.BlockSpec((N, N), whole, pipeline_mode=pl.Buffered(1)),
            ]
            + [pl.BlockSpec((edge, N), whole, pipeline_mode=pl.Buffered(1))] * 4
            + [pl.BlockSpec(memory_space=pl.ANY)] * 2,
            out_specs=[
                pl.BlockSpec((CHUNK, N), lambda i, *_: (i, 0)),
                pl.BlockSpec((PACK, B), whole),
            ],
            scratch_shapes=[
                pltpu.VMEM((rows + 4 * edge, N), BF16),
                pltpu.VMEM((rows + 4 * edge, N), BF16),
                pltpu.VMEM((CHUNK, 3 * N), BF16),
                pltpu.VMEM((CHUNK, 2 * N), BF16),
                pltpu.VMEM((4, N, N), F32),
                pltpu.VMEM((8, N), F32),
                pltpu.SemaphoreType.DMA((2,)),
            ],
        ),
        out_shape=[
            jax.ShapeDtypeStruct((rows, N), F32),
            jax.ShapeDtypeStruct((PACK, B), F32),
        ],
        compiler_params=pltpu.CompilerParams(vmem_limit_bytes=40 << 20),
        cost_estimate=pl.CostEstimate(flops=24 * rows * N * N, bytes_accessed=16 * rows * N, transcendentals=0),
        name="image",
    )(index_map, tangent, forcing, gram_local, *halos, sh, sl)


PARTS = 3
PART = PACK // PARTS
STAGE_SLOTS = (1, 3, 3, 3, 3, 3, 1)
STAGE_BASE = tuple(PARTS * sum(STAGE_SLOTS[:i]) for i in range(7))


def reduce_kernel(x_ref, o_ref, acc1, acc2, got0, got1, got2, got3, send_sem, recv_sem):
    rows_id = lax.axis_index("rows")
    zone_id = lax.axis_index("zone")
    core = zone_id % 2
    place = {"x": zone_id // 2, "y": rows_id % 4, "z": rows_id // 4}
    orders = (("x", "y", "z"), ("y", "z", "x"), ("z", "x", "y"))

    def device(axis, shift):
        at = dict(place)
        if axis == "core":
            return (rows_id, at["x"] * 2 + (1 - core))
        at[axis] = (at[axis] + shift) % 4
        return (at["z"] * 4 + at["y"], at["x"] * 2 + core)

    barrier = pltpu.get_barrier_semaphore()
    for axis, shift in [("core", 1)] + [(a, s) for a in "xyz" for s in (1, 2, 3)]:
        pl.semaphore_signal(barrier, inc=1, device_id=device(axis, shift), device_id_type=MESH)
    pl.semaphore_wait(barrier, 10)

    live = {}

    def send(stage, part, slot, src, dst, axis, shift):
        k = STAGE_BASE[stage] + part * STAGE_SLOTS[stage] + slot
        copy = pltpu.make_async_remote_copy(
            src_ref=src, dst_ref=dst, send_sem=send_sem.at[k], recv_sem=recv_sem.at[k],
            device_id=device(axis, shift), device_id_type=MESH,
        )
        copy.start()
        live[stage, part, slot] = copy

    def arrive(stage, part):
        for slot in range(STAGE_SLOTS[stage]):
            live[stage, part, slot].wait_recv()

    half = PART // 2
    quarter = half // 4
    piece = quarter // 4
    mine = core * half
    for p in range(PARTS):
        send(0, p, 0, x_ref.at[pl.ds(p * PART + (1 - core) * half, half)], got0.at[p], "core", 1)
    for p, (a, b, c) in enumerate(orders):
        arrive(0, p)
        acc1[p] = x_ref[pl.ds(p * PART + mine, half), :] + got0[p]
        for o in (1, 2, 3):
            there = (place[a] + o) % 4
            send(1, p, o - 1, acc1.at[p, pl.ds(there * quarter, quarter)], got1.at[p, o - 1], a, o)
    for p, (a, b, c) in enumerate(orders):
        arrive(1, p)
        acc2[p] = acc1[p, pl.ds(place[a] * quarter, quarter), :] + got1[p, 0] + got1[p, 1] + got1[p, 2]
        for o in (1, 2, 3):
            there = (place[b] + o) % 4
            send(2, p, o - 1, acc2.at[p, pl.ds(there * piece, piece)], got2.at[p, o - 1], b, o)
    for p, (a, b, c) in enumerate(orders):
        arrive(2, p)
        got3[p, place[c]] = acc2[p, pl.ds(place[b] * piece, piece), :] + got2[p, 0] + got2[p, 1] + got2[p, 2]
        for o in (1, 2, 3):
            send(3, p, o - 1, got3.at[p, place[c]], got3.at[p, place[c]], c, o)
    for p, (a, b, c) in enumerate(orders):
        arrive(3, p)
        spot = p * PART + mine + place[a] * quarter + place[b] * piece
        o_ref[pl.ds(spot, piece), :] = got3[p, 0] + got3[p, 1] + got3[p, 2] + got3[p, 3]
        for o in (1, 2, 3):
            send(4, p, o - 1, o_ref.at[pl.ds(spot, piece)], o_ref.at[pl.ds(spot, piece)], b, o)
    for p, (a, b, c) in enumerate(orders):
        arrive(4, p)
        spot = p * PART + mine + place[a] * quarter
        for o in (1, 2, 3):
            send(5, p, o - 1, o_ref.at[pl.ds(spot, quarter)], o_ref.at[pl.ds(spot, quarter)], a, o)
    for p in range(PARTS):
        arrive(5, p)
        spot = p * PART + mine
        send(6, p, 0, o_ref.at[pl.ds(spot, half)], o_ref.at[pl.ds(spot, half)], "core", 1)
    for p in range(PARTS):
        arrive(6, p)
    for copy in live.values():
        copy.wait_send()


def reduce_all(pack):
    half = PART // 2
    count = PARTS * sum(STAGE_SLOTS)
    return pl.pallas_call(
        reduce_kernel,
        out_shape=jax.ShapeDtypeStruct((PACK, B), F32),
        in_specs=[pl.BlockSpec(memory_space=pltpu.VMEM)],
        out_specs=pl.BlockSpec(memory_space=pltpu.VMEM),
        scratch_shapes=[
            pltpu.VMEM((PARTS, half, B), F32),
            pltpu.VMEM((PARTS, half // 4, B), F32),
            pltpu.VMEM((PARTS, half, B), F32),
            pltpu.VMEM((PARTS, 3, half // 4, B), F32),
            pltpu.VMEM((PARTS, 3, half // 16, B), F32),
            pltpu.VMEM((PARTS, 4, half // 16, B), F32),
            pltpu.SemaphoreType.DMA((count,)),
            pltpu.SemaphoreType.DMA((count,)),
        ],
        compiler_params=pltpu.CompilerParams(collective_id=0, has_side_effects=True, vmem_limit_bytes=16 << 20),
        name="reduce_all",
    )(pack)


def factor_blocks(matrices):
    tiles = [[m[8 * t : 8 * t + 8, :] for t in range(16)] for m in matrices]
    lane = lax.broadcasted_iota(jnp.int32, (8, B), 1)
    sub = lax.broadcasted_iota(jnp.int32, (8, B), 0)
    inverse = [[(lane == sub + 8 * t).astype(F32) for t in range(16)] for _ in matrices]
    for k in range(B):
        t0, i = divmod(k, 8)
        for a, e in zip(tiles, inverse):
            pivot = lax.rsqrt(a[t0][i : i + 1, k : k + 1])
            row = a[t0][i : i + 1, :] * pivot
            erow = e[t0][i : i + 1, :] * pivot
            for t in range(t0, 16):
                scale = a[t][:, k : k + 1] * pivot
                new_a = a[t] - scale * row
                new_e = e[t] - scale * erow
                if t == t0:
                    new_a = jnp.where(sub > i, new_a, jnp.where(sub == i, row, a[t]))
                    new_e = jnp.where(sub > i, new_e, jnp.where(sub == i, erow, e[t]))
                a[t] = new_a
                e[t] = new_e
    upper = [
        jnp.concatenate([jnp.where(lane >= sub + 8 * t, a[t], 0.0) for t in range(16)], axis=0) for a in tiles
    ]
    return upper, [jnp.concatenate(e, axis=0) for e in inverse]


def dotf(a, b, dims):
    return lax.dot_general(a, b, ((dims[:1], dims[1:]), ((), ())), precision=HI, preferred_element_type=F32)


def split3(x):
    hi = x.astype(BF16)
    rest = x - hi.astype(F32)
    mid = rest.astype(BF16)
    return hi, mid, (rest - mid.astype(F32)).astype(BF16)


def row_dot(a, b, dims):
    left, right = split3(a), split3(b)
    total = jnp.zeros((8, N), F32)
    for i, j in ((2, 0), (1, 1), (0, 2), (1, 0), (0, 1), (0, 0)):
        total += lax.dot_general(
            left[i], right[j], ((dims[:1], dims[1:]), ((), ())), preferred_element_type=F32
        )
    return total


def solve_kernel(x_ref, step_ref, wh_ref, wl_ref, d_ref, c_ref, now):
    scale = 1.0 / (8192 * 128)
    block = lambda i: x_ref[i * B : (i + 1) * B, :] * scale
    g11, g12, g22, n11, n12, n22 = (block(i) for i in range(6))
    (u_g, u_n), (e_g, e_n) = factor_blocks([g11, n11])
    u12_g = dotf(e_g, g12, (1, 0))
    u12_n = dotf(e_n, n12, (1, 0))
    s_g = g22 - dotf(u12_g, u12_g, (0, 0))
    s_n = n22 - dotf(u12_n, u12_n, (0, 0))
    (v_g, v_n), (h_g, h_n) = factor_blocks([s_g, s_n])
    low_g = -dotf(h_g, dotf(u12_g, e_g, (0, 0)), (1, 0))
    low_n = -dotf(h_n, dotf(u12_n, e_n, (0, 0)), (1, 0))
    zero = jnp.zeros((B, B), F32)
    weight = jnp.concatenate(
        [jnp.concatenate([e_g.T, low_g.T], axis=1), jnp.concatenate([zero, h_g.T], axis=1)], axis=0
    )
    hi, lo = split(weight)
    wh_ref[...] = hi
    wl_ref[...] = lo
    inv_n = jnp.concatenate(
        [jnp.concatenate([e_n, zero], axis=1), jnp.concatenate([low_n, h_n], axis=1)], axis=0
    )
    upper = jnp.concatenate(
        [jnp.concatenate([u_g, u12_g], axis=1), jnp.concatenate([zero, v_g], axis=1)], axis=0
    )
    project = jnp.concatenate(
        [jnp.concatenate([block(6), block(7)], axis=1), jnp.concatenate([block(8), block(9)], axis=1)], axis=0
    )
    load = jnp.concatenate([x_ref[10 * B : 10 * B + 1, :], x_ref[10 * B + 1 : 10 * B + 2, :]], axis=1)
    load = jnp.broadcast_to(load * (scale * STEP), (8, N))
    turn = dotf(dotf(project, inv_n, (0, 1)), inv_n, (1, 0))
    shift = row_dot(row_dot(load, inv_n, (1, 1)), inv_n, (1, 0))
    index = step_ref[...]
    state = (index == jnp.max(index, axis=1, keepdims=True)).astype(F32)
    now[...] = jnp.broadcast_to(state, (8, N))
    d_ref[...] = jnp.zeros((8, N), F32)
    for i in range(STEPS):
        now[...] = row_dot(now[...], turn, (1, 0)) + shift
        d_ref[i : i + 1, :] = now[:1, :]
    c_ref[...] = row_dot(d_ref[...], upper, (1, 1))[:STEPS, :]


def reduced(total, step_index):
    return pl.pallas_call(
        solve_kernel,
        out_shape=[
            jax.ShapeDtypeStruct((N, N), BF16),
            jax.ShapeDtypeStruct((N, N), BF16),
            jax.ShapeDtypeStruct((8, N), F32),
            jax.ShapeDtypeStruct((STEPS, N), F32),
        ],
        in_specs=[pl.BlockSpec(memory_space=pltpu.VMEM)] * 2,
        out_specs=[pl.BlockSpec(memory_space=pltpu.VMEM)] * 4,
        scratch_shapes=[pltpu.VMEM((8, N), F32)],
        compiler_params=pltpu.CompilerParams(vmem_limit_bytes=24 << 20),
        name="reduced",
    )(total, step_index.reshape(1, N))


def final_kernel(s_ref, y_ref, f_ref, wh_ref, wl_ref, d_ref, basis_ref, res_ref, acc):
    step = pl.program_id(0)
    s = s_ref[...]
    hi, lo = split(s)
    wh = wh_ref[...]
    out = jnp.dot(hi, wh, preferred_element_type=F32)
    out += jnp.dot(lo, wh, preferred_element_type=F32)
    out += jnp.dot(hi, wl_ref[...], preferred_element_type=F32)
    basis_ref[...] = out
    last = d_ref[2:3, :]
    before = d_ref[1:2, :]
    lane = lax.broadcasted_iota(jnp.int32, (B, B), 1)
    for g in range(CHUNK // B):
        rows = slice(g * B, (g + 1) * B)
        z = y_ref[rows, :] * last - s[rows, :] * before
        z = jnp.sum(z[:, :B] + z[:, B:], axis=1, keepdims=True)
        acc[...] = jnp.where(lane == g, z, acc[...])
    res_ref[...] = acc[...].T[: CHUNK // B, :] - STEP * f_ref[...]


def final(snapshots, y, forcing, wh, wl, d):
    rows = snapshots.shape[0]
    whole = lambda i: (0, 0)
    return pl.pallas_call(
        final_kernel,
        grid=(rows // CHUNK,),
        in_specs=[
            pl.BlockSpec((CHUNK, N), lambda i: (i, 0)),
            pl.BlockSpec((CHUNK, N), lambda i: (i, 0)),
            pl.BlockSpec((CHUNK // B, B), lambda i: (i, 0)),
            pl.BlockSpec((N, N), whole),
            pl.BlockSpec((N, N), whole),
            pl.BlockSpec((8, N), whole),
        ],
        out_specs=[
            pl.BlockSpec((CHUNK, N), lambda i: (i, 0)),
            pl.BlockSpec((CHUNK // B, B), lambda i: (i, 0)),
        ],
        out_shape=[
            jax.ShapeDtypeStruct((rows, N), F32),
            jax.ShapeDtypeStruct((rows // B, B), F32),
        ],
        scratch_shapes=[pltpu.VMEM((B, B), F32)],
        compiler_params=pltpu.CompilerParams(vmem_limit_bytes=24 << 20),
        cost_estimate=pl.CostEstimate(flops=6 * rows * N * N, bytes_accessed=12 * rows * N, transcendentals=0),
        name="final",
    )(snapshots, y, forcing, wh, wl, d)


def shifted(value, axis, steps, wrap):
    count = lax.axis_size(axis)
    pairs = [(i, (i + steps) % count) for i in range(count) if wrap or 0 <= i + steps < count]
    return lax.ppermute(value, axis, pairs)


def shards(snapshots, tangent, pattern, forcing, step_index):
    rows = snapshots.shape[0]
    blocks = rows // B
    edge = HALO * B
    tail = snapshots[rows - edge :]
    head = snapshots[:edge]
    halos = (
        shifted(tail, "rows", 1, True),
        shifted(head, "rows", -1, True),
        shifted(tail, "zone", 1, False),
        shifted(head, "zone", -1, False),
    )
    source = pattern // blocks
    block = pattern % blocks
    tail_side = (source == 1) | (source == 3)
    index_map = jnp.where(
        source == 0, block, blocks + HALO * (source - 1) + block - jnp.where(tail_side, blocks - HALO, 0)
    )
    sh, sl, gram_local = gram(snapshots)
    force = forcing.reshape(blocks, B)
    y, pack = image(index_map, tangent, force, gram_local, halos, sh, sl)
    total = reduce_all(pack)
    wh, wl, d, coefficients = reduced(total, step_index)
    basis, residual = final(snapshots, y, force, wh, wl, d)
    return basis, coefficients, residual.reshape(rows)


def solution(mesh):
    both = ("rows", "zone")
    in_specs = (P(both, None), P(both, None), P(both, None), P(both), P())
    out_specs = (P(both, None), P(), P(both))
    return jax.shard_map(shards, mesh=mesh, in_specs=in_specs, out_specs=out_specs, check_vma=False)
```

```python
import functools

import jax
import jax.numpy as jnp
from jax import lax
from jax.experimental import pallas as pl
from jax.experimental.pallas import tpu as pltpu
from jax.sharding import PartitionSpec as P

HALO = 4
STEPS = 3
STEP = 0.25
B = 128
N = 256
CHUNK = 1024
PACK = 1536
F32 = jnp.float32
BF16 = jnp.bfloat16
HI = lax.Precision.HIGHEST
MESH = pl.DeviceIdType.MESH


def split(x):
    hi = x.astype(BF16)
    return hi, (x - hi.astype(F32)).astype(BF16)


def tdot(a, b):
    return lax.dot_general(a, b, (((0,), (0,)), ((), ())), preferred_element_type=F32)


def front_kernel(s_hbm, ch_ref, cl_ref, g_ref, sbuf, halo, load_sem, send_sem, recv_sem):
    rows = s_hbm.shape[0]
    edge = HALO * B
    chunks = rows // CHUNK
    ring, belt = lax.axis_size("rows"), lax.axis_size("zone")
    row_id, zone_id = lax.axis_index("rows"), lax.axis_index("zone")
    loads = []
    for i in range(chunks):
        part = pl.ds(i * CHUNK, CHUNK)
        loads.append(pltpu.make_async_copy(s_hbm.at[part], sbuf.at[part], load_sem.at[i]))
        loads[-1].start()
    peers = (
        ((row_id + 1) % ring, zone_id),
        ((row_id + ring - 1) % ring, zone_id),
        (row_id, (zone_id + 1) % belt),
        (row_id, (zone_id + belt - 1) % belt),
    )
    barrier = pltpu.get_barrier_semaphore()
    for peer in peers:
        pl.semaphore_signal(barrier, inc=1, device_id=peer, device_id_type=MESH)
    pl.semaphore_wait(barrier, 4)
    copies = []
    for i, peer in enumerate(peers):
        start = rows - edge if i % 2 == 0 else 0
        copies.append(
            pltpu.make_async_remote_copy(
                src_ref=s_hbm.at[pl.ds(start, edge)], dst_ref=halo.at[i],
                send_sem=send_sem.at[i], recv_sem=recv_sem.at[i], device_id=peer, device_id_type=MESH,
            )
        )
        copies[-1].start()
    total = jnp.zeros((N, N), F32)
    for i in range(chunks):
        loads[i].wait()
        part = pl.ds(i * CHUNK, CHUNK)
        hi, lo = split(sbuf[part, :])
        ch_ref[part, :] = hi
        cl_ref[part, :] = lo
        total += tdot(hi, hi)
    g_ref[...] = total
    there = (True, True, zone_id > 0, zone_id < belt - 1)
    for i in (2, 3, 0, 1):
        copies[i].wait_recv()
        value = halo[i]
        if i >= 2:
            value = jnp.where(there[i], value, 0.0)
        hi, lo = split(value)
        part = pl.ds(rows + i * edge, edge)
        ch_ref[part, :] = hi
        cl_ref[part, :] = lo
    for copy in copies:
        copy.wait_send()


def front(snapshots):
    rows = snapshots.shape[0]
    edge = HALO * B
    return pl.pallas_call(
        front_kernel,
        in_specs=[pl.BlockSpec(memory_space=pl.ANY)],
        out_specs=[pl.BlockSpec(memory_space=pltpu.VMEM)] * 3,
        out_shape=[
            jax.ShapeDtypeStruct((rows + 4 * edge, N), BF16),
            jax.ShapeDtypeStruct((rows + 4 * edge, N), BF16),
            jax.ShapeDtypeStruct((N, N), F32),
        ],
        scratch_shapes=[
            pltpu.VMEM((rows, N), F32),
            pltpu.VMEM((4, edge, N), F32),
            pltpu.SemaphoreType.DMA((rows // CHUNK,)),
            pltpu.SemaphoreType.DMA((4,)),
            pltpu.SemaphoreType.DMA((4,)),
        ],
        compiler_params=pltpu.CompilerParams(collective_id=1, has_side_effects=True, vmem_limit_bytes=38 << 20),
        cost_estimate=pl.CostEstimate(flops=2 * rows * N * N, bytes_accessed=8 * rows * N, transcendentals=0),
        name="front",
    )(snapshots)


def image_kernel(
    index_ref, t_ref, f_ref, g_ref, cand_h, cand_l, y_ref, pack_ref, left, right, acc, load_acc,
):
    step = pl.program_id(0)

    @pl.when(step == 0)
    def _():
        acc[...] = jnp.zeros_like(acc)
        load_acc[...] = jnp.zeros_like(load_acc)

    groups = CHUNK // B
    force = f_ref[...].T
    total = jnp.zeros((8, N), F32)
    for g in range(groups):
        picks = [pl.ds(pl.multiple_of(index_ref[step * groups + g, e] * B, B), B) for e in range(4)]
        tiles = t_ref[g * B : (g + 1) * B, :]
        image = jnp.dot(tiles, jnp.concatenate([cand_h[p, :] for p in picks], axis=0), preferred_element_type=F32)
        image += jnp.dot(tiles, jnp.concatenate([cand_l[p, :] for p in picks], axis=0), preferred_element_type=F32)
        own = pl.ds(pl.multiple_of(step * CHUNK + g * B, B), B)
        y = cand_h[own, :].astype(F32) + cand_l[own, :].astype(F32) + STEP * image
        y_ref[own, :] = y
        hi, lo = split(y)
        left[g * B : (g + 1) * B, :N] = hi
        left[g * B : (g + 1) * B, N : 2 * N] = lo
        right[g * B : (g + 1) * B, N:] = hi
        total += jnp.sum((y * force[:, g : g + 1]).reshape(B // 8, 8, N), axis=0)
    load_acc[...] += total
    here = pl.ds(pl.multiple_of(step * CHUNK, CHUNK), CHUNK)
    left[:, 2 * N :] = cand_l[here, :]
    right[:, :N] = cand_h[here, :]
    both = tdot(left[...], right[...])
    acc[0] += both[:N, :N] + both[N : 2 * N, :N]
    acc[1] += both[:N, N:] * 0.5 + both[N : 2 * N, N:]
    acc[2] += both[2 * N :, N:]
    acc[3] += both[2 * N :, :N]

    @pl.when(step == pl.num_programs(0) - 1)
    def _():
        normal = acc[1] + acc[1].T
        project = acc[0] + acc[2].T
        half = g_ref[...] * 0.5 + acc[3]
        gram_matrix = half + half.T
        blocks = []
        for matrix in (gram_matrix, normal):
            blocks += [matrix[:B, :B], matrix[:B, B:], matrix[B:, B:]]
        blocks += [project[:B, :B], project[:B, B:], project[B:, :B], project[B:, B:]]
        for i, block in enumerate(blocks):
            pack_ref[i * B : (i + 1) * B, :] = block
        load = jnp.sum(load_acc[...], axis=0, keepdims=True)
        pack_ref[10 * B :, :] = jnp.zeros((PACK - 10 * B, B), F32)
        pack_ref[10 * B : 10 * B + 1, :] = load[:, :B]
        pack_ref[10 * B + 1 : 10 * B + 2, :] = load[:, B:]


def image(index_map, tangent, forcing, gram_local, cand_h, cand_l):
    rows = tangent.shape[0]
    whole = lambda i, *_: (0, 0)
    return pl.pallas_call(
        image_kernel,
        grid_spec=pltpu.PrefetchScalarGridSpec(
            num_scalar_prefetch=1,
            grid=(rows // CHUNK,),
            in_specs=[
                pl.BlockSpec((CHUNK, 4 * B), lambda i, *_: (i, 0)),
                pl.BlockSpec((CHUNK // B, B), lambda i, *_: (i, 0)),
                pl.BlockSpec(memory_space=pltpu.VMEM),
                pl.BlockSpec(memory_space=pltpu.VMEM),
                pl.BlockSpec(memory_space=pltpu.VMEM),
            ],
            out_specs=[
                pl.BlockSpec(memory_space=pltpu.VMEM),
                pl.BlockSpec((PACK, B), whole),
            ],
            scratch_shapes=[
                pltpu.VMEM((CHUNK, 3 * N), BF16),
                pltpu.VMEM((CHUNK, 2 * N), BF16),
                pltpu.VMEM((4, N, N), F32),
                pltpu.VMEM((8, N), F32),
            ],
        ),
        out_shape=[
            jax.ShapeDtypeStruct((rows, N), F32),
            jax.ShapeDtypeStruct((PACK, B), F32),
        ],
        compiler_params=pltpu.CompilerParams(vmem_limit_bytes=28 << 20),
        cost_estimate=pl.CostEstimate(flops=20 * rows * N * N, bytes_accessed=8 * rows * N, transcendentals=0),
        name="image",
    )(index_map, tangent, forcing, gram_local, cand_h, cand_l)


PARTS = 3
PART = PACK // PARTS
STAGE_SLOTS = (1, 3, 3, 3, 3, 3, 1)
STAGE_BASE = tuple(PARTS * sum(STAGE_SLOTS[:i]) for i in range(7))


def reduce_kernel(x_ref, o_ref, acc1, acc2, got0, got1, got2, got3, send_sem, recv_sem):
    rows_id = lax.axis_index("rows")
    zone_id = lax.axis_index("zone")
    core = zone_id % 2
    place = {"x": zone_id // 2, "y": rows_id % 4, "z": rows_id // 4}
    orders = (("x", "y", "z"), ("y", "z", "x"), ("z", "x", "y"))

    def device(axis, shift):
        at = dict(place)
        if axis == "core":
            return (rows_id, at["x"] * 2 + (1 - core))
        at[axis] = (at[axis] + shift) % 4
        return (at["z"] * 4 + at["y"], at["x"] * 2 + core)

    barrier = pltpu.get_barrier_semaphore()
    for axis, shift in [("core", 1)] + [(a, s) for a in "xyz" for s in (1, 2, 3)]:
        pl.semaphore_signal(barrier, inc=1, device_id=device(axis, shift), device_id_type=MESH)
    pl.semaphore_wait(barrier, 10)

    live = {}

    def send(stage, part, slot, src, dst, axis, shift):
        k = STAGE_BASE[stage] + part * STAGE_SLOTS[stage] + slot
        copy = pltpu.make_async_remote_copy(
            src_ref=src, dst_ref=dst, send_sem=send_sem.at[k], recv_sem=recv_sem.at[k],
            device_id=device(axis, shift), device_id_type=MESH,
        )
        copy.start()
        live[stage, part, slot] = copy

    def arrive(stage, part):
        for slot in range(STAGE_SLOTS[stage]):
            live[stage, part, slot].wait_recv()

    half = PART // 2
    quarter = half // 4
    piece = quarter // 4
    mine = core * half
    for p in range(PARTS):
        send(0, p, 0, x_ref.at[pl.ds(p * PART + (1 - core) * half, half)], got0.at[p], "core", 1)
    for p, (a, b, c) in enumerate(orders):
        arrive(0, p)
        acc1[p] = x_ref[pl.ds(p * PART + mine, half), :] + got0[p]
        for o in (1, 2, 3):
            there = (place[a] + o) % 4
            send(1, p, o - 1, acc1.at[p, pl.ds(there * quarter, quarter)], got1.at[p, o - 1], a, o)
    for p, (a, b, c) in enumerate(orders):
        arrive(1, p)
        acc2[p] = acc1[p, pl.ds(place[a] * quarter, quarter), :] + got1[p, 0] + got1[p, 1] + got1[p, 2]
        for o in (1, 2, 3):
            there = (place[b] + o) % 4
            send(2, p, o - 1, acc2.at[p, pl.ds(there * piece, piece)], got2.at[p, o - 1], b, o)
    for p, (a, b, c) in enumerate(orders):
        arrive(2, p)
        got3[p, place[c]] = acc2[p, pl.ds(place[b] * piece, piece), :] + got2[p, 0] + got2[p, 1] + got2[p, 2]
        for o in (1, 2, 3):
            send(3, p, o - 1, got3.at[p, place[c]], got3.at[p, place[c]], c, o)
    for p, (a, b, c) in enumerate(orders):
        arrive(3, p)
        spot = p * PART + mine + place[a] * quarter + place[b] * piece
        o_ref[pl.ds(spot, piece), :] = got3[p, 0] + got3[p, 1] + got3[p, 2] + got3[p, 3]
        for o in (1, 2, 3):
            send(4, p, o - 1, o_ref.at[pl.ds(spot, piece)], o_ref.at[pl.ds(spot, piece)], b, o)
    for p, (a, b, c) in enumerate(orders):
        arrive(4, p)
        spot = p * PART + mine + place[a] * quarter
        for o in (1, 2, 3):
            send(5, p, o - 1, o_ref.at[pl.ds(spot, quarter)], o_ref.at[pl.ds(spot, quarter)], a, o)
    for p in range(PARTS):
        arrive(5, p)
        spot = p * PART + mine
        send(6, p, 0, o_ref.at[pl.ds(spot, half)], o_ref.at[pl.ds(spot, half)], "core", 1)
    for p in range(PARTS):
        arrive(6, p)
    for copy in live.values():
        copy.wait_send()


def reduce_all(pack):
    half = PART // 2
    count = PARTS * sum(STAGE_SLOTS)
    return pl.pallas_call(
        reduce_kernel,
        out_shape=jax.ShapeDtypeStruct((PACK, B), F32),
        in_specs=[pl.BlockSpec(memory_space=pltpu.VMEM)],
        out_specs=pl.BlockSpec(memory_space=pltpu.VMEM),
        scratch_shapes=[
            pltpu.VMEM((PARTS, half, B), F32),
            pltpu.VMEM((PARTS, half // 4, B), F32),
            pltpu.VMEM((PARTS, half, B), F32),
            pltpu.VMEM((PARTS, 3, half // 4, B), F32),
            pltpu.VMEM((PARTS, 3, half // 16, B), F32),
            pltpu.VMEM((PARTS, 4, half // 16, B), F32),
            pltpu.SemaphoreType.DMA((count,)),
            pltpu.SemaphoreType.DMA((count,)),
        ],
        compiler_params=pltpu.CompilerParams(collective_id=0, has_side_effects=True, vmem_limit_bytes=16 << 20),
        name="reduce_all",
    )(pack)


def factor_blocks(matrices):
    tiles = [[m[8 * t : 8 * t + 8, :] for t in range(16)] for m in matrices]
    lane = lax.broadcasted_iota(jnp.int32, (8, B), 1)
    sub = lax.broadcasted_iota(jnp.int32, (8, B), 0)
    inverse = [[(lane == sub + 8 * t).astype(F32) for t in range(16)] for _ in matrices]
    for k in range(B):
        t0, i = divmod(k, 8)
        for a, e in zip(tiles, inverse):
            pivot = lax.rsqrt(a[t0][i : i + 1, k : k + 1])
            row = a[t0][i : i + 1, :] * pivot
            erow = e[t0][i : i + 1, :] * pivot
            for t in range(t0, 16):
                scale = a[t][:, k : k + 1] * pivot
                new_a = a[t] - scale * row
                new_e = e[t] - scale * erow
                if t == t0:
                    new_a = jnp.where(sub > i, new_a, jnp.where(sub == i, row, a[t]))
                    new_e = jnp.where(sub > i, new_e, jnp.where(sub == i, erow, e[t]))
                a[t] = new_a
                e[t] = new_e
    upper = [
        jnp.concatenate([jnp.where(lane >= sub + 8 * t, a[t], 0.0) for t in range(16)], axis=0) for a in tiles
    ]
    return upper, [jnp.concatenate(e, axis=0) for e in inverse]


def dotf(a, b, dims):
    return lax.dot_general(a, b, ((dims[:1], dims[1:]), ((), ())), precision=HI, preferred_element_type=F32)


def split3(x):
    hi = x.astype(BF16)
    rest = x - hi.astype(F32)
    mid = rest.astype(BF16)
    return hi, mid, (rest - mid.astype(F32)).astype(BF16)


def row_dot(a, b, dims):
    left, right = split3(a), split3(b)
    total = jnp.zeros((8, N), F32)
    for i, j in ((2, 0), (1, 1), (0, 2), (1, 0), (0, 1), (0, 0)):
        total += lax.dot_general(
            left[i], right[j], ((dims[:1], dims[1:]), ((), ())), preferred_element_type=F32
        )
    return total


def solve_kernel(x_ref, step_ref, wh_ref, wl_ref, d_ref, c_ref, now):
    scale = 1.0 / (8192 * 128)
    block = lambda i: x_ref[i * B : (i + 1) * B, :] * scale
    g11, g12, g22, n11, n12, n22 = (block(i) for i in range(6))
    (u_g, u_n), (e_g, e_n) = factor_blocks([g11, n11])
    u12_g = dotf(e_g, g12, (1, 0))
    u12_n = dotf(e_n, n12, (1, 0))
    s_g = g22 - dotf(u12_g, u12_g, (0, 0))
    s_n = n22 - dotf(u12_n, u12_n, (0, 0))
    (v_g, v_n), (h_g, h_n) = factor_blocks([s_g, s_n])
    low_g = -dotf(h_g, dotf(u12_g, e_g, (0, 0)), (1, 0))
    low_n = -dotf(h_n, dotf(u12_n, e_n, (0, 0)), (1, 0))
    zero = jnp.zeros((B, B), F32)
    weight = jnp.concatenate(
        [jnp.concatenate([e_g.T, low_g.T], axis=1), jnp.concatenate([zero, h_g.T], axis=1)], axis=0
    )
    hi, lo = split(weight)
    wh_ref[...] = hi
    wl_ref[...] = lo
    inv_n = jnp.concatenate(
        [jnp.concatenate([e_n, zero], axis=1), jnp.concatenate([low_n, h_n], axis=1)], axis=0
    )
    upper = jnp.concatenate(
        [jnp.concatenate([u_g, u12_g], axis=1), jnp.concatenate([zero, v_g], axis=1)], axis=0
    )
    project = jnp.concatenate(
        [jnp.concatenate([block(6), block(7)], axis=1), jnp.concatenate([block(8), block(9)], axis=1)], axis=0
    )
    load = jnp.concatenate([x_ref[10 * B : 10 * B + 1, :], x_ref[10 * B + 1 : 10 * B + 2, :]], axis=1)
    load = jnp.broadcast_to(load * (scale * STEP), (8, N))
    turn = dotf(dotf(project, inv_n, (0, 1)), inv_n, (1, 0))
    shift = row_dot(row_dot(load, inv_n, (1, 1)), inv_n, (1, 0))
    index = step_ref[...]
    state = (index == jnp.max(index, axis=1, keepdims=True)).astype(F32)
    now[...] = jnp.broadcast_to(state, (8, N))
    d_ref[...] = jnp.zeros((8, N), F32)
    for i in range(STEPS):
        now[...] = row_dot(now[...], turn, (1, 0)) + shift
        d_ref[i : i + 1, :] = now[:1, :]
    c_ref[...] = row_dot(d_ref[...], upper, (1, 1))[:STEPS, :]


def reduced(total, step_index):
    return pl.pallas_call(
        solve_kernel,
        out_shape=[
            jax.ShapeDtypeStruct((N, N), BF16),
            jax.ShapeDtypeStruct((N, N), BF16),
            jax.ShapeDtypeStruct((8, N), F32),
            jax.ShapeDtypeStruct((STEPS, N), F32),
        ],
        in_specs=[pl.BlockSpec(memory_space=pltpu.VMEM)] * 2,
        out_specs=[pl.BlockSpec(memory_space=pltpu.VMEM)] * 4,
        scratch_shapes=[pltpu.VMEM((8, N), F32)],
        compiler_params=pltpu.CompilerParams(vmem_limit_bytes=24 << 20),
        name="reduced",
    )(total, step_index.reshape(1, N))


def final_kernel(ch_ref, cl_ref, y_ref, f_ref, wh_ref, wl_ref, d_ref, basis_ref, res_ref, acc):
    step = pl.program_id(0)
    here = pl.ds(pl.multiple_of(step * CHUNK, CHUNK), CHUNK)
    hi = ch_ref[here, :]
    lo = cl_ref[here, :]
    wh = wh_ref[...]
    out = jnp.dot(hi, wh, preferred_element_type=F32)
    out += jnp.dot(lo, wh, preferred_element_type=F32)
    out += jnp.dot(hi, wl_ref[...], preferred_element_type=F32)
    basis_ref[...] = out
    last = d_ref[2:3, :]
    before = d_ref[1:2, :]
    lane = lax.broadcasted_iota(jnp.int32, (B, B), 1)
    for g in range(CHUNK // B):
        own = pl.ds(pl.multiple_of(step * CHUNK + g * B, B), B)
        s = ch_ref[own, :].astype(F32) + cl_ref[own, :].astype(F32)
        z = y_ref[own, :] * last - s * before
        z = jnp.sum(z[:, :B] + z[:, B:], axis=1, keepdims=True)
        acc[...] = jnp.where(lane == g, z, acc[...])
    res_ref[...] = acc[...].T[: CHUNK // B, :] - STEP * f_ref[...]


def final(cand_h, cand_l, y, forcing, wh, wl, d):
    rows = y.shape[0]
    whole = lambda i: (0, 0)
    return pl.pallas_call(
        final_kernel,
        grid=(rows // CHUNK,),
        in_specs=[pl.BlockSpec(memory_space=pltpu.VMEM)] * 3
        + [
            pl.BlockSpec((CHUNK // B, B), lambda i: (i, 0)),
            pl.BlockSpec((N, N), whole),
            pl.BlockSpec((N, N), whole),
            pl.BlockSpec((8, N), whole),
        ],
        out_specs=[
            pl.BlockSpec((CHUNK, N), lambda i: (i, 0)),
            pl.BlockSpec((CHUNK // B, B), lambda i: (i, 0)),
        ],
        out_shape=[
            jax.ShapeDtypeStruct((rows, N), F32),
            jax.ShapeDtypeStruct((rows // B, B), F32),
        ],
        scratch_shapes=[pltpu.VMEM((B, B), F32)],
        compiler_params=pltpu.CompilerParams(vmem_limit_bytes=28 << 20),
        cost_estimate=pl.CostEstimate(flops=6 * rows * N * N, bytes_accessed=12 * rows * N, transcendentals=0),
        name="final",
    )(cand_h, cand_l, y, forcing, wh, wl, d)


def shards(snapshots, tangent, pattern, forcing, step_index):
    rows = snapshots.shape[0]
    blocks = rows // B
    source = pattern // blocks
    block = pattern % blocks
    tail_side = (source == 1) | (source == 3)
    index_map = jnp.where(
        source == 0, block, blocks + HALO * (source - 1) + block - jnp.where(tail_side, blocks - HALO, 0)
    )
    cand_h, cand_l, gram_local = front(snapshots)
    force = forcing.reshape(blocks, B)
    y, pack = image(index_map, tangent, force, gram_local, cand_h, cand_l)
    total = reduce_all(pack)
    wh, wl, d, coefficients = reduced(total, step_index)
    basis, residual = final(cand_h, cand_l, y, force, wh, wl, d)
    return basis, coefficients, residual.reshape(rows)


def solution(mesh):
    both = ("rows", "zone")
    in_specs = (P(both, None), P(both, None), P(both, None), P(both), P())
    out_specs = (P(both, None), P(), P(both))
    return jax.shard_map(shards, mesh=mesh, in_specs=in_specs, out_specs=out_specs, check_vma=False)
```

```python
import functools

import jax
import jax.numpy as jnp
from jax import lax
from jax.experimental import pallas as pl
from jax.experimental.pallas import tpu as pltpu
from jax.sharding import PartitionSpec as P

HALO = 4
STEPS = 3
STEP = 0.25
B = 128
N = 256
CHUNK = 1024
PACK = 1344
F32 = jnp.float32
BF16 = jnp.bfloat16
HI = lax.Precision.HIGHEST
MESH = pl.DeviceIdType.MESH


def split(x):
    hi = x.astype(BF16)
    return hi, (x - hi.astype(F32)).astype(BF16)


def tdot(a, b):
    return lax.dot_general(a, b, (((0,), (0,)), ((), ())), preferred_element_type=F32)


def front_kernel(s_hbm, ch_ref, cl_ref, g_ref, sbuf, halo, load_sem, send_sem, recv_sem):
    rows = s_hbm.shape[0]
    edge = HALO * B
    chunks = rows // CHUNK
    ring, belt = lax.axis_size("rows"), lax.axis_size("zone")
    row_id, zone_id = lax.axis_index("rows"), lax.axis_index("zone")
    loads = []
    for i in range(chunks):
        part = pl.ds(i * CHUNK, CHUNK)
        loads.append(pltpu.make_async_copy(s_hbm.at[part], sbuf.at[part], load_sem.at[i]))
        loads[-1].start()
    peers = (
        ((row_id + 1) % ring, zone_id),
        ((row_id + ring - 1) % ring, zone_id),
        (row_id, (zone_id + 1) % belt),
        (row_id, (zone_id + belt - 1) % belt),
    )
    barrier = pltpu.get_barrier_semaphore()
    for peer in peers:
        pl.semaphore_signal(barrier, inc=1, device_id=peer, device_id_type=MESH)
    pl.semaphore_wait(barrier, 4)
    copies = []
    for i, peer in enumerate(peers):
        start = rows - edge if i % 2 == 0 else 0
        copies.append(
            pltpu.make_async_remote_copy(
                src_ref=s_hbm.at[pl.ds(start, edge)], dst_ref=halo.at[i],
                send_sem=send_sem.at[i], recv_sem=recv_sem.at[i], device_id=peer, device_id_type=MESH,
            )
        )
        copies[-1].start()
    total = jnp.zeros((2 * N, N), F32)
    for i in range(chunks):
        loads[i].wait()
        part = pl.ds(i * CHUNK, CHUNK)
        hi, lo = split(sbuf[part, :])
        ch_ref[part, :] = hi
        cl_ref[part, :] = lo
        total += tdot(jnp.concatenate([hi, lo], axis=1), hi)
    half = total[:N] * 0.5 + total[N:]
    g_ref[...] = half + half.T
    there = (True, True, zone_id > 0, zone_id < belt - 1)
    for i in (2, 3, 0, 1):
        copies[i].wait_recv()
        value = halo[i]
        if i >= 2:
            value = jnp.where(there[i], value, 0.0)
        hi, lo = split(value)
        part = pl.ds(rows + i * edge, edge)
        ch_ref[part, :] = hi
        cl_ref[part, :] = lo
    for copy in copies:
        copy.wait_send()


def front(snapshots):
    rows = snapshots.shape[0]
    edge = HALO * B
    return pl.pallas_call(
        front_kernel,
        in_specs=[pl.BlockSpec(memory_space=pl.ANY)],
        out_specs=[pl.BlockSpec(memory_space=pltpu.VMEM)] * 3,
        out_shape=[
            jax.ShapeDtypeStruct((rows + 4 * edge, N), BF16),
            jax.ShapeDtypeStruct((rows + 4 * edge, N), BF16),
            jax.ShapeDtypeStruct((N, N), F32),
        ],
        scratch_shapes=[
            pltpu.VMEM((rows, N), F32),
            pltpu.VMEM((4, edge, N), F32),
            pltpu.SemaphoreType.DMA((rows // CHUNK,)),
            pltpu.SemaphoreType.DMA((4,)),
            pltpu.SemaphoreType.DMA((4,)),
        ],
        compiler_params=pltpu.CompilerParams(collective_id=1, has_side_effects=True, vmem_limit_bytes=38 << 20),
        cost_estimate=pl.CostEstimate(flops=2 * rows * N * N, bytes_accessed=8 * rows * N, transcendentals=0),
        name="front",
    )(snapshots)


def image_kernel(
    index_ref, t_ref, f_ref, g_ref, cand_h, cand_l, y_ref, pack_ref, ybuf_h, ybuf_l, acc, load_acc,
):
    step = pl.program_id(0)

    @pl.when(step == 0)
    def _():
        acc[...] = jnp.zeros_like(acc)
        load_acc[...] = jnp.zeros_like(load_acc)

    groups = CHUNK // B
    force = f_ref[...].T
    total = jnp.zeros((8, N), F32)
    for g in range(groups):
        picks = [pl.ds(pl.multiple_of(index_ref[step * groups + g, e] * B, B), B) for e in range(4)]
        tiles = t_ref[g * B : (g + 1) * B, :]
        image = jnp.dot(tiles, jnp.concatenate([cand_h[p, :] for p in picks], axis=0), preferred_element_type=F32)
        image += jnp.dot(tiles, jnp.concatenate([cand_l[p, :] for p in picks], axis=0), preferred_element_type=F32)
        own = pl.ds(pl.multiple_of(step * CHUNK + g * B, B), B)
        y = cand_h[own, :].astype(F32) + cand_l[own, :].astype(F32) + STEP * image
        y_ref[own, :] = y
        hi, lo = split(y)
        ybuf_h[g * B : (g + 1) * B, :] = hi
        ybuf_l[g * B : (g + 1) * B, :] = lo
        total += jnp.sum((y * force[:, g : g + 1]).reshape(B // 8, 8, N), axis=0)
    load_acc[...] += total
    here = pl.ds(pl.multiple_of(step * CHUNK, CHUNK), CHUNK)
    yh = ybuf_h[...]
    yl = ybuf_l[...]
    one = tdot(jnp.concatenate([yh, yl], axis=1), cand_h[here, :])
    acc[0] += one[:N] + one[N:]
    two = tdot(jnp.concatenate([yh, yl, cand_l[here, :]], axis=1), yh)
    acc[1] += two[:N] * 0.5 + two[N : 2 * N]
    acc[2] += two[2 * N :]

    @pl.when(step == pl.num_programs(0) - 1)
    def _():
        normal = acc[1] + acc[1].T
        project = acc[0] + acc[2].T
        gram_matrix = g_ref[...]
        blocks = []
        for matrix in (gram_matrix, normal):
            blocks += [matrix[:B, :B], matrix[:B, B:], matrix[B:, B:]]
        blocks += [project[:B, :B], project[:B, B:], project[B:, :B], project[B:, B:]]
        for i, block in enumerate(blocks):
            pack_ref[i * B : (i + 1) * B, :] = block
        load = jnp.sum(load_acc[...], axis=0, keepdims=True)
        pack_ref[10 * B :, :] = jnp.zeros((PACK - 10 * B, B), F32)
        pack_ref[10 * B : 10 * B + 1, :] = load[:, :B]
        pack_ref[10 * B + 1 : 10 * B + 2, :] = load[:, B:]


def image(index_map, tangent, forcing, gram_local, cand_h, cand_l):
    rows = tangent.shape[0]
    whole = lambda i, *_: (0, 0)
    return pl.pallas_call(
        image_kernel,
        grid_spec=pltpu.PrefetchScalarGridSpec(
            num_scalar_prefetch=1,
            grid=(rows // CHUNK,),
            in_specs=[
                pl.BlockSpec((CHUNK, 4 * B), lambda i, *_: (i, 0)),
                pl.BlockSpec((CHUNK // B, B), lambda i, *_: (i, 0)),
                pl.BlockSpec(memory_space=pltpu.VMEM),
                pl.BlockSpec(memory_space=pltpu.VMEM),
                pl.BlockSpec(memory_space=pltpu.VMEM),
            ],
            out_specs=[
                pl.BlockSpec(memory_space=pltpu.VMEM),
                pl.BlockSpec((PACK, B), whole),
            ],
            scratch_shapes=[
                pltpu.VMEM((CHUNK, N), BF16),
                pltpu.VMEM((CHUNK, N), BF16),
                pltpu.VMEM((3, N, N), F32),
                pltpu.VMEM((8, N), F32),
            ],
        ),
        out_shape=[
            jax.ShapeDtypeStruct((rows, N), F32),
            jax.ShapeDtypeStruct((PACK, B), F32),
        ],
        compiler_params=pltpu.CompilerParams(vmem_limit_bytes=28 << 20),
        cost_estimate=pl.CostEstimate(flops=20 * rows * N * N, bytes_accessed=8 * rows * N, transcendentals=0),
        name="image",
    )(index_map, tangent, forcing, gram_local, cand_h, cand_l)


PARTS = 3
PART = PACK // PARTS
STAGE_SLOTS = (1, 3, 3, 3, 3, 1)
STAGE_BASE = tuple(PARTS * sum(STAGE_SLOTS[:i]) for i in range(6))


def reduce_kernel(x_ref, o_ref, acc, got0, got1, got2, got3, send_sem, recv_sem):
    rows_id = lax.axis_index("rows")
    zone_id = lax.axis_index("zone")
    core = zone_id % 2
    place = {"x": zone_id // 2, "y": rows_id % 4, "z": rows_id // 4}
    orders = (("x", "y", "z"), ("y", "z", "x"), ("z", "x", "y"))

    def device(axis, shift):
        at = dict(place)
        if axis == "core":
            return (rows_id, at["x"] * 2 + (1 - core))
        at[axis] = (at[axis] + shift) % 4
        return (at["z"] * 4 + at["y"], at["x"] * 2 + core)

    barrier = pltpu.get_barrier_semaphore()
    for axis, shift in [("core", 1)] + [(a, s) for a in "xyz" for s in (1, 2, 3)]:
        pl.semaphore_signal(barrier, inc=1, device_id=device(axis, shift), device_id_type=MESH)
    pl.semaphore_wait(barrier, 10)

    live = {}

    def send(stage, part, slot, src, dst, axis, shift):
        k = STAGE_BASE[stage] + part * STAGE_SLOTS[stage] + slot
        copy = pltpu.make_async_remote_copy(
            src_ref=src, dst_ref=dst, send_sem=send_sem.at[k], recv_sem=recv_sem.at[k],
            device_id=device(axis, shift), device_id_type=MESH,
        )
        copy.start()
        live[stage, part, slot] = copy

    def arrive(stage, part):
        for slot in range(STAGE_SLOTS[stage]):
            live[stage, part, slot].wait_recv()

    half = PART // 2
    quarter = half // 4
    mine = core * half
    for p in range(PARTS):
        send(0, p, 0, x_ref.at[pl.ds(p * PART + (1 - core) * half, half)], got0.at[p], "core", 1)
    for p, (a, b, c) in enumerate(orders):
        arrive(0, p)
        acc[p] = x_ref[pl.ds(p * PART + mine, half), :] + got0[p]
        for o in (1, 2, 3):
            there = (place[a] + o) % 4
            send(1, p, o - 1, acc.at[p, pl.ds(there * quarter, quarter)], got1.at[p, o - 1], a, o)
    for p, (a, b, c) in enumerate(orders):
        arrive(1, p)
        slot = got2.at[p, place[b]]
        slot[...] = acc[p, pl.ds(place[a] * quarter, quarter), :] + got1[p, 0] + got1[p, 1] + got1[p, 2]
        for o in (1, 2, 3):
            send(2, p, o - 1, slot, slot, b, o)
    for p, (a, b, c) in enumerate(orders):
        arrive(2, p)
        slot = got3.at[p, place[c]]
        slot[...] = got2[p, 0] + got2[p, 1] + got2[p, 2] + got2[p, 3]
        for o in (1, 2, 3):
            send(3, p, o - 1, slot, slot, c, o)
    for p, (a, b, c) in enumerate(orders):
        arrive(3, p)
        spot = o_ref.at[pl.ds(p * PART + mine + place[a] * quarter, quarter)]
        spot[...] = got3[p, 0] + got3[p, 1] + got3[p, 2] + got3[p, 3]
        for o in (1, 2, 3):
            send(4, p, o - 1, spot, spot, a, o)
    for p in range(PARTS):
        arrive(4, p)
        spot = o_ref.at[pl.ds(p * PART + mine, half)]
        send(5, p, 0, spot, spot, "core", 1)
    for p in range(PARTS):
        arrive(5, p)
    for copy in live.values():
        copy.wait_send()


def reduce_all(pack):
    half = PART // 2
    count = PARTS * sum(STAGE_SLOTS)
    return pl.pallas_call(
        reduce_kernel,
        out_shape=jax.ShapeDtypeStruct((PACK, B), F32),
        in_specs=[pl.BlockSpec(memory_space=pltpu.VMEM)],
        out_specs=pl.BlockSpec(memory_space=pltpu.VMEM),
        scratch_shapes=[
            pltpu.VMEM((PARTS, half, B), F32),
            pltpu.VMEM((PARTS, half, B), F32),
            pltpu.VMEM((PARTS, 3, half // 4, B), F32),
            pltpu.VMEM((PARTS, 4, half // 4, B), F32),
            pltpu.VMEM((PARTS, 4, half // 4, B), F32),
            pltpu.SemaphoreType.DMA((count,)),
            pltpu.SemaphoreType.DMA((count,)),
        ],
        compiler_params=pltpu.CompilerParams(collective_id=0, has_side_effects=True, vmem_limit_bytes=16 << 20),
        name="reduce_all",
    )(pack)


def split3f(x):
    hi = x.astype(BF16).astype(F32)
    mid = (x - hi).astype(BF16).astype(F32)
    return hi, mid, (x - hi - mid)


def factor_blocks(matrices):
    tiles = [[m[8 * t : 8 * t + 8, :] for t in range(16)] for m in matrices]
    lane = lax.broadcasted_iota(jnp.int32, (8, B), 1)
    sub = lax.broadcasted_iota(jnp.int32, (8, B), 0)
    inverse = [[(lane == sub + 8 * t).astype(F32) for t in range(16)] for _ in matrices]
    for p in range(16):
        for a, e in zip(tiles, inverse):
            spread = lambda t: [jnp.broadcast_to(a[t][:, 8 * p + c : 8 * p + c + 1], (8, B)) for c in range(8)]
            column = spread(p)
            pivot, link = [], {}
            for k in range(8):
                pivot.append(lax.rsqrt(column[k][k : k + 1, :]))
                column[k] = column[k] * pivot[k]
                for c in range(k + 1, 8):
                    link[k, c] = column[k][c : c + 1, :]
                    column[c] = column[c] - column[k] * link[k, c]
            rows, erows = [], []
            own, eown = a[p], e[p]
            for k in range(8):
                rows.append(own[k : k + 1, :] * pivot[k])
                erows.append(eown[k : k + 1, :] * pivot[k])
                own = own - column[k] * rows[k]
                eown = eown - column[k] * erows[k]
            if p + 1 < 16:
                t = p + 1
                column = spread(t)
                for k in range(8):
                    column[k] = column[k] * pivot[k]
                    for c in range(k + 1, 8):
                        column[c] = column[c] - column[k] * link[k, c]
                    a[t] = a[t] - column[k] * rows[k]
                    e[t] = e[t] - column[k] * erows[k]
            a[p] = jnp.concatenate(rows, axis=0)
            e[p] = jnp.concatenate(erows, axis=0)
            if p + 2 < 16:
                ah, am, al = split3f(a[p])
                eh, em, el = split3f(e[p])
                lhs = jnp.concatenate([ah, ah, am, ah, al, am], axis=0).astype(BF16)
                rhs = jnp.concatenate(
                    [jnp.concatenate([ah, am, ah, al, ah, am], axis=0), jnp.concatenate([eh, em, eh, el, eh, em], axis=0)], axis=1
                ).astype(BF16)
                update = tdot(lhs, rhs)
                for t in range(p + 2, 16):
                    a[t] = a[t] - update[8 * t : 8 * t + 8, :B]
                    e[t] = e[t] - update[8 * t : 8 * t + 8, B:]
    upper = [
        jnp.concatenate([jnp.where(lane >= sub + 8 * t, a[t], 0.0) for t in range(16)], axis=0) for a in tiles
    ]
    return upper, [jnp.concatenate(e, axis=0) for e in inverse]


def dotf(a, b, dims):
    return lax.dot_general(a, b, ((dims[:1], dims[1:]), ((), ())), precision=HI, preferred_element_type=F32)


def split3(x):
    hi = x.astype(BF16)
    rest = x - hi.astype(F32)
    mid = rest.astype(BF16)
    return hi, mid, (rest - mid.astype(F32)).astype(BF16)


def row_dot(a, b, dims):
    left, right = split3(a), split3(b)
    total = jnp.zeros((8, N), F32)
    for i, j in ((2, 0), (1, 1), (0, 2), (1, 0), (0, 1), (0, 0)):
        total += lax.dot_general(
            left[i], right[j], ((dims[:1], dims[1:]), ((), ())), preferred_element_type=F32
        )
    return total


def solve_kernel(x_ref, step_ref, wh_ref, wl_ref, d_ref, c_ref, now):
    scale = 1.0 / (8192 * 128)
    block = lambda i: x_ref[i * B : (i + 1) * B, :] * scale
    g11, g12, g22, n11, n12, n22 = (block(i) for i in range(6))
    (u_g, u_n), (e_g, e_n) = factor_blocks([g11, n11])
    u12_g = dotf(e_g, g12, (1, 0))
    u12_n = dotf(e_n, n12, (1, 0))
    s_g = g22 - dotf(u12_g, u12_g, (0, 0))
    s_n = n22 - dotf(u12_n, u12_n, (0, 0))
    (v_g, v_n), (h_g, h_n) = factor_blocks([s_g, s_n])
    low_g = -dotf(h_g, dotf(u12_g, e_g, (0, 0)), (1, 0))
    low_n = -dotf(h_n, dotf(u12_n, e_n, (0, 0)), (1, 0))
    zero = jnp.zeros((B, B), F32)
    weight = jnp.concatenate(
        [jnp.concatenate([e_g.T, low_g.T], axis=1), jnp.concatenate([zero, h_g.T], axis=1)], axis=0
    )
    hi, lo = split(weight)
    wh_ref[...] = hi
    wl_ref[...] = lo
    inv_n = jnp.concatenate(
        [jnp.concatenate([e_n, zero], axis=1), jnp.concatenate([low_n, h_n], axis=1)], axis=0
    )
    upper = jnp.concatenate(
        [jnp.concatenate([u_g, u12_g], axis=1), jnp.concatenate([zero, v_g], axis=1)], axis=0
    )
    project = jnp.concatenate(
        [jnp.concatenate([block(6), block(7)], axis=1), jnp.concatenate([block(8), block(9)], axis=1)], axis=0
    )
    load = jnp.concatenate([x_ref[10 * B : 10 * B + 1, :], x_ref[10 * B + 1 : 10 * B + 2, :]], axis=1)
    stack = jnp.concatenate([project.T, jnp.broadcast_to(load * (scale * STEP), (8, N))], axis=0)
    stack = dotf(dotf(stack, inv_n, (1, 1)), inv_n, (1, 0))
    turn = stack[:N]
    shift = stack[N:]
    index = step_ref[...]
    state = (index == jnp.max(index, axis=1, keepdims=True)).astype(F32)
    now[...] = jnp.broadcast_to(state, (8, N))
    d_ref[...] = jnp.zeros((8, N), F32)
    for i in range(STEPS):
        now[...] = row_dot(now[...], turn, (1, 0)) + shift
        d_ref[i : i + 1, :] = now[:1, :]
    c_ref[...] = row_dot(d_ref[...], upper, (1, 1))[:STEPS, :]


def reduced(total, step_index):
    return pl.pallas_call(
        solve_kernel,
        out_shape=[
            jax.ShapeDtypeStruct((N, N), BF16),
            jax.ShapeDtypeStruct((N, N), BF16),
            jax.ShapeDtypeStruct((8, N), F32),
            jax.ShapeDtypeStruct((STEPS, N), F32),
        ],
        in_specs=[pl.BlockSpec(memory_space=pltpu.VMEM)] * 2,
        out_specs=[pl.BlockSpec(memory_space=pltpu.VMEM)] * 4,
        scratch_shapes=[pltpu.VMEM((8, N), F32)],
        compiler_params=pltpu.CompilerParams(vmem_limit_bytes=24 << 20),
        name="reduced",
    )(total, step_index.reshape(1, N))


def final_kernel(ch_ref, cl_ref, y_ref, f_ref, wh_ref, wl_ref, d_ref, basis_ref, res_ref, acc):
    step = pl.program_id(0)
    here = pl.ds(pl.multiple_of(step * CHUNK, CHUNK), CHUNK)
    hi = ch_ref[here, :]
    lo = cl_ref[here, :]
    wh = wh_ref[...]
    out = jnp.dot(hi, wh, preferred_element_type=F32)
    out += jnp.dot(lo, wh, preferred_element_type=F32)
    out += jnp.dot(hi, wl_ref[...], preferred_element_type=F32)
    basis_ref[...] = out
    last = d_ref[2:3, :]
    before = d_ref[1:2, :]
    lane = lax.broadcasted_iota(jnp.int32, (B, B), 1)
    for g in range(CHUNK // B):
        own = pl.ds(pl.multiple_of(step * CHUNK + g * B, B), B)
        s = ch_ref[own, :].astype(F32) + cl_ref[own, :].astype(F32)
        z = y_ref[own, :] * last - s * before
        z = jnp.sum(z[:, :B] + z[:, B:], axis=1, keepdims=True)
        acc[...] = jnp.where(lane == g, z, acc[...])
    res_ref[...] = acc[...].T[: CHUNK // B, :] - STEP * f_ref[...]


def final(cand_h, cand_l, y, forcing, wh, wl, d):
    rows = y.shape[0]
    whole = lambda i: (0, 0)
    return pl.pallas_call(
        final_kernel,
        grid=(rows // CHUNK,),
        in_specs=[pl.BlockSpec(memory_space=pltpu.VMEM)] * 3
        + [
            pl.BlockSpec((CHUNK // B, B), lambda i: (i, 0)),
            pl.BlockSpec((N, N), whole),
            pl.BlockSpec((N, N), whole),
            pl.BlockSpec((8, N), whole),
        ],
        out_specs=[
            pl.BlockSpec((CHUNK, N), lambda i: (i, 0)),
            pl.BlockSpec((CHUNK // B, B), lambda i: (i, 0)),
        ],
        out_shape=[
            jax.ShapeDtypeStruct((rows, N), F32),
            jax.ShapeDtypeStruct((rows // B, B), F32),
        ],
        scratch_shapes=[pltpu.VMEM((B, B), F32)],
        compiler_params=pltpu.CompilerParams(vmem_limit_bytes=28 << 20),
        cost_estimate=pl.CostEstimate(flops=6 * rows * N * N, bytes_accessed=12 * rows * N, transcendentals=0),
        name="final",
    )(cand_h, cand_l, y, forcing, wh, wl, d)


def shards(snapshots, tangent, pattern, forcing, step_index):
    rows = snapshots.shape[0]
    blocks = rows // B
    source = pattern // blocks
    block = pattern % blocks
    tail_side = (source == 1) | (source == 3)
    index_map = jnp.where(
        source == 0, block, blocks + HALO * (source - 1) + block - jnp.where(tail_side, blocks - HALO, 0)
    )
    cand_h, cand_l, gram_local = front(snapshots)
    force = forcing.reshape(blocks, B)
    y, pack = image(index_map, tangent, force, gram_local, cand_h, cand_l)
    total = reduce_all(pack)
    wh, wl, d, coefficients = reduced(total, step_index)
    basis, residual = final(cand_h, cand_l, y, force, wh, wl, d)
    return basis, coefficients, residual.reshape(rows)


def solution(mesh):
    both = ("rows", "zone")
    in_specs = (P(both, None), P(both, None), P(both, None), P(both), P())
    out_specs = (P(both, None), P(), P(both))
    return jax.shard_map(shards, mesh=mesh, in_specs=in_specs, out_specs=out_specs, check_vma=False)
```

```python
import functools

import jax
import jax.numpy as jnp
from jax import lax
from jax.experimental import pallas as pl
from jax.experimental.pallas import tpu as pltpu
from jax.sharding import PartitionSpec as P

HALO = 4
STEPS = 3
STEP = 0.25
B = 128
N = 256
CHUNK = 1024
PACK = 1344
F32 = jnp.float32
BF16 = jnp.bfloat16
HI = lax.Precision.HIGHEST
MESH = pl.DeviceIdType.MESH


def split(x):
    hi = x.astype(BF16)
    return hi, (x - hi.astype(F32)).astype(BF16)


def tdot(a, b):
    return lax.dot_general(a, b, (((0,), (0,)), ((), ())), preferred_element_type=F32)


def front_kernel(s_hbm, ch_ref, cl_ref, g_ref, sbuf, halo, load_sem, send_sem, recv_sem):
    rows = s_hbm.shape[0]
    edge = HALO * B
    chunks = rows // CHUNK
    ring, belt = lax.axis_size("rows"), lax.axis_size("zone")
    row_id, zone_id = lax.axis_index("rows"), lax.axis_index("zone")
    loads = []
    for i in range(chunks):
        part = pl.ds(i * CHUNK, CHUNK)
        loads.append(pltpu.make_async_copy(s_hbm.at[part], sbuf.at[part], load_sem.at[i]))
        loads[-1].start()
    peers = (
        ((row_id + 1) % ring, zone_id),
        ((row_id + ring - 1) % ring, zone_id),
        (row_id, (zone_id + 1) % belt),
        (row_id, (zone_id + belt - 1) % belt),
    )
    barrier = pltpu.get_barrier_semaphore()
    for peer in peers:
        pl.semaphore_signal(barrier, inc=1, device_id=peer, device_id_type=MESH)
    pl.semaphore_wait(barrier, 4)
    copies = []
    for i, peer in enumerate(peers):
        start = rows - edge if i % 2 == 0 else 0
        copies.append(
            pltpu.make_async_remote_copy(
                src_ref=s_hbm.at[pl.ds(start, edge)], dst_ref=halo.at[i],
                send_sem=send_sem.at[i], recv_sem=recv_sem.at[i], device_id=peer, device_id_type=MESH,
            )
        )
        copies[-1].start()
    total = jnp.zeros((2 * N, N), F32)
    for i in range(chunks):
        loads[i].wait()
        part = pl.ds(i * CHUNK, CHUNK)
        hi, lo = split(sbuf[part, :])
        spot = pl.ds(i * CHUNK // B, CHUNK // B)
        ch_ref[spot] = hi.reshape(CHUNK // B, B, N)
        cl_ref[spot] = lo.reshape(CHUNK // B, B, N)
        total += tdot(jnp.concatenate([hi, lo], axis=1), hi)
    half = total[:N] * 0.5 + total[N:]
    g_ref[...] = half + half.T
    there = (True, True, zone_id > 0, zone_id < belt - 1)
    for i in (2, 3, 0, 1):
        copies[i].wait_recv()
        value = halo[i]
        if i >= 2:
            value = jnp.where(there[i], value, 0.0)
        hi, lo = split(value)
        spot = pl.ds(rows // B + i * HALO, HALO)
        ch_ref[spot] = hi.reshape(HALO, B, N)
        cl_ref[spot] = lo.reshape(HALO, B, N)
    for copy in copies:
        copy.wait_send()


def front(snapshots):
    rows = snapshots.shape[0]
    edge = HALO * B
    return pl.pallas_call(
        front_kernel,
        in_specs=[pl.BlockSpec(memory_space=pl.ANY)],
        out_specs=[pl.BlockSpec(memory_space=pltpu.VMEM)] * 3,
        out_shape=[
            jax.ShapeDtypeStruct((rows // B + 4 * HALO, B, N), BF16),
            jax.ShapeDtypeStruct((rows // B + 4 * HALO, B, N), BF16),
            jax.ShapeDtypeStruct((N, N), F32),
        ],
        scratch_shapes=[
            pltpu.VMEM((rows, N), F32),
            pltpu.VMEM((4, edge, N), F32),
            pltpu.SemaphoreType.DMA((rows // CHUNK,)),
            pltpu.SemaphoreType.DMA((4,)),
            pltpu.SemaphoreType.DMA((4,)),
        ],
        compiler_params=pltpu.CompilerParams(collective_id=1, has_side_effects=True, vmem_limit_bytes=38 << 20),
        cost_estimate=pl.CostEstimate(flops=2 * rows * N * N, bytes_accessed=8 * rows * N, transcendentals=0),
        name="front",
    )(snapshots)


PARTS = 3
PART = PACK // PARTS
STAGE_SLOTS = (1, 3, 3, 3, 3, 1)
STAGE_BASE = tuple(PARTS * sum(STAGE_SLOTS[:i]) for i in range(6))


def reach():
    rows_id = lax.axis_index("rows")
    zone_id = lax.axis_index("zone")
    core = zone_id % 2
    place = {"x": zone_id // 2, "y": rows_id % 4, "z": rows_id // 4}
    def device(axis, shift):
        at = dict(place)
        if axis == "core":
            return (rows_id, at["x"] * 2 + (1 - core))
        at[axis] = (at[axis] + shift) % 4
        return (at["z"] * 4 + at["y"], at["x"] * 2 + core)

    return core, place, device


def greet():
    _, _, device = reach()
    barrier = pltpu.get_barrier_semaphore()
    for axis, shift in [("core", 1)] + [(a, s) for a in "xyz" for s in (1, 2, 3)]:
        pl.semaphore_signal(barrier, inc=1, device_id=device(axis, shift), device_id_type=MESH)


def reduce_all(x_ref, o_ref, acc, got0, got1, got2, got3, send_sem, recv_sem):
    core, place, device = reach()
    pl.semaphore_wait(pltpu.get_barrier_semaphore(), 10)
    live = {}

    def send(stage, part, slot, src, dst, axis, shift):
        k = STAGE_BASE[stage] + part * STAGE_SLOTS[stage] + slot
        copy = pltpu.make_async_remote_copy(
            src_ref=src, dst_ref=dst, send_sem=send_sem.at[k], recv_sem=recv_sem.at[k],
            device_id=device(axis, shift), device_id_type=MESH,
        )
        copy.start()
        live[stage, part, slot] = copy

    def arrive(stage, part):
        for slot in range(STAGE_SLOTS[stage]):
            live[stage, part, slot].wait_recv()

    orders = (("x", "y", "z"), ("y", "z", "x"), ("z", "x", "y"))
    half = PART // 2
    quarter = half // 4
    mine = core * half
    for p in range(PARTS):
        send(0, p, 0, x_ref.at[pl.ds(p * PART + (1 - core) * half, half)], got0.at[p], "core", 1)
    for p, (a, b, c) in enumerate(orders):
        arrive(0, p)
        acc[p] = x_ref[pl.ds(p * PART + mine, half), :] + got0[p]
        for o in (1, 2, 3):
            there = (place[a] + o) % 4
            send(1, p, o - 1, acc.at[p, pl.ds(there * quarter, quarter)], got1.at[p, o - 1], a, o)
    for p, (a, b, c) in enumerate(orders):
        arrive(1, p)
        slot = got2.at[p, place[b]]
        slot[...] = acc[p, pl.ds(place[a] * quarter, quarter), :] + got1[p, 0] + got1[p, 1] + got1[p, 2]
        for o in (1, 2, 3):
            send(2, p, o - 1, slot, slot, b, o)
    for p, (a, b, c) in enumerate(orders):
        arrive(2, p)
        slot = got3.at[p, place[c]]
        slot[...] = got2[p, 0] + got2[p, 1] + got2[p, 2] + got2[p, 3]
        for o in (1, 2, 3):
            send(3, p, o - 1, slot, slot, c, o)
    for p, (a, b, c) in enumerate(orders):
        arrive(3, p)
        spot = o_ref.at[pl.ds(p * PART + mine + place[a] * quarter, quarter)]
        spot[...] = got3[p, 0] + got3[p, 1] + got3[p, 2] + got3[p, 3]
        for o in (1, 2, 3):
            send(4, p, o - 1, spot, spot, a, o)
    for p in range(PARTS):
        arrive(4, p)
        spot = o_ref.at[pl.ds(p * PART + mine, half)]
        send(5, p, 0, spot, spot, "core", 1)
    for p in range(PARTS):
        arrive(5, p)
    for copy in live.values():
        copy.wait_send()


def image_kernel(
    index_ref, t_ref, f_ref, g_ref, cand_h, cand_l, y_ref, total_ref,
    ybuf_h, ybuf_l, acc, load_acc, pack_ref, *exchange,
):
    step = pl.program_id(0)

    @pl.when(step == 0)
    def _():
        greet()
        acc[...] = jnp.zeros_like(acc)
        load_acc[...] = jnp.zeros_like(load_acc)

    groups = CHUNK // B
    force = f_ref[...].T
    total = jnp.zeros((8, N), F32)
    for g in range(groups):
        picks = [index_ref[e, step * groups + g] for e in range(4)]
        tiles = t_ref[g * B : (g + 1) * B, :]
        image = jnp.dot(tiles, jnp.concatenate([cand_h[p] for p in picks], axis=0), preferred_element_type=F32)
        image += jnp.dot(tiles, jnp.concatenate([cand_l[p] for p in picks], axis=0), preferred_element_type=F32)
        own = pl.ds(pl.multiple_of(step * CHUNK + g * B, B), B)
        y = cand_h[step * groups + g].astype(F32) + cand_l[step * groups + g].astype(F32) + STEP * image
        y_ref[own, :] = y
        hi, lo = split(y)
        ybuf_h[g * B : (g + 1) * B, :] = hi
        ybuf_l[g * B : (g + 1) * B, :] = lo
        total += jnp.sum((y * force[:, g : g + 1]).reshape(B // 8, 8, N), axis=0)
    load_acc[...] += total
    here = pl.ds(step * groups, groups)
    yh = ybuf_h[...]
    yl = ybuf_l[...]
    one = tdot(jnp.concatenate([yh, yl], axis=1), cand_h[here].reshape(CHUNK, N))
    acc[0] += one[:N] + one[N:]
    two = tdot(jnp.concatenate([yh, yl, cand_l[here].reshape(CHUNK, N)], axis=1), yh)
    acc[1] += two[:N] * 0.5 + two[N : 2 * N]
    acc[2] += two[2 * N :]

    @pl.when(step == pl.num_programs(0) - 1)
    def _():
        normal = acc[1] + acc[1].T
        project = acc[0] + acc[2].T
        gram_matrix = g_ref[...]
        blocks = []
        for matrix in (gram_matrix, normal):
            blocks += [matrix[:B, :B], matrix[:B, B:], matrix[B:, B:]]
        blocks += [project[:B, :B], project[:B, B:], project[B:, :B], project[B:, B:]]
        for i, block in enumerate(blocks):
            pack_ref[i * B : (i + 1) * B, :] = block
        load = jnp.sum(load_acc[...], axis=0, keepdims=True)
        pack_ref[10 * B :, :] = jnp.zeros((PACK - 10 * B, B), F32)
        pack_ref[10 * B : 10 * B + 1, :] = load[:, :B]
        pack_ref[10 * B + 1 : 10 * B + 2, :] = load[:, B:]
        reduce_all(pack_ref, *exchange)
        total_ref[...] = exchange[0][...]


def image(index_map, tangent, forcing, gram_local, cand_h, cand_l):
    rows = tangent.shape[0]
    half = PART // 2
    count = PARTS * sum(STAGE_SLOTS)
    return pl.pallas_call(
        image_kernel,
        grid_spec=pltpu.PrefetchScalarGridSpec(
            num_scalar_prefetch=1,
            grid=(rows // CHUNK,),
            in_specs=[
                pl.BlockSpec((CHUNK, 4 * B), lambda i, *_: (i, 0)),
                pl.BlockSpec((CHUNK // B, B), lambda i, *_: (i, 0)),
                pl.BlockSpec(memory_space=pltpu.VMEM),
                pl.BlockSpec(memory_space=pltpu.VMEM),
                pl.BlockSpec(memory_space=pltpu.VMEM),
            ],
            out_specs=[
                pl.BlockSpec(memory_space=pltpu.VMEM),
                pl.BlockSpec(memory_space=pltpu.VMEM),
            ],
            scratch_shapes=[
                pltpu.VMEM((CHUNK, N), BF16),
                pltpu.VMEM((CHUNK, N), BF16),
                pltpu.VMEM((3, N, N), F32),
                pltpu.VMEM((8, N), F32),
                pltpu.VMEM((PACK, B), F32),
                pltpu.VMEM((PACK, B), F32),
                pltpu.VMEM((PARTS, half, B), F32),
                pltpu.VMEM((PARTS, half, B), F32),
                pltpu.VMEM((PARTS, 3, half // 4, B), F32),
                pltpu.VMEM((PARTS, 4, half // 4, B), F32),
                pltpu.VMEM((PARTS, 4, half // 4, B), F32),
                pltpu.SemaphoreType.DMA((count,)),
                pltpu.SemaphoreType.DMA((count,)),
            ],
        ),
        out_shape=[
            jax.ShapeDtypeStruct((rows, N), F32),
            jax.ShapeDtypeStruct((PACK, B), F32),
        ],
        compiler_params=pltpu.CompilerParams(collective_id=0, has_side_effects=True, vmem_limit_bytes=28 << 20),
        cost_estimate=pl.CostEstimate(flops=20 * rows * N * N, bytes_accessed=8 * rows * N, transcendentals=0),
        name="image",
    )(index_map, tangent, forcing, gram_local, cand_h, cand_l)


def split3f(x):
    hi = x.astype(BF16).astype(F32)
    mid = (x - hi).astype(BF16).astype(F32)
    return hi, mid, (x - hi - mid)


def factor_blocks(matrices):
    tiles = [[m[8 * t : 8 * t + 8, :] for t in range(16)] for m in matrices]
    lane = lax.broadcasted_iota(jnp.int32, (8, B), 1)
    sub = lax.broadcasted_iota(jnp.int32, (8, B), 0)
    inverse = [[(lane == sub + 8 * t).astype(F32) for t in range(16)] for _ in matrices]
    for p in range(16):
        for a, e in zip(tiles, inverse):
            spread = lambda t: [jnp.broadcast_to(a[t][:, 8 * p + c : 8 * p + c + 1], (8, B)) for c in range(8)]
            column = spread(p)
            pivot, link = [], {}
            for k in range(8):
                pivot.append(lax.rsqrt(column[k][k : k + 1, :]))
                column[k] = column[k] * pivot[k]
                for c in range(k + 1, 8):
                    link[k, c] = column[k][c : c + 1, :]
                    column[c] = column[c] - column[k] * link[k, c]
            rows, erows = [], []
            own, eown = a[p], e[p]
            for k in range(8):
                rows.append(own[k : k + 1, :] * pivot[k])
                erows.append(eown[k : k + 1, :] * pivot[k])
                own = own - column[k] * rows[k]
                eown = eown - column[k] * erows[k]
            if p + 1 < 16:
                t = p + 1
                column = spread(t)
                for k in range(8):
                    column[k] = column[k] * pivot[k]
                    for c in range(k + 1, 8):
                        column[c] = column[c] - column[k] * link[k, c]
                    a[t] = a[t] - column[k] * rows[k]
                    e[t] = e[t] - column[k] * erows[k]
            a[p] = jnp.concatenate(rows, axis=0)
            e[p] = jnp.concatenate(erows, axis=0)
            if p + 2 < 16:
                ah, am, al = split3f(a[p])
                eh, em, el = split3f(e[p])
                lhs = jnp.concatenate([ah, ah, am, ah, al, am], axis=0).astype(BF16)
                rhs = jnp.concatenate(
                    [jnp.concatenate([ah, am, ah, al, ah, am], axis=0), jnp.concatenate([eh, em, eh, el, eh, em], axis=0)], axis=1
                ).astype(BF16)
                update = tdot(lhs, rhs)
                for t in range(p + 2, 16):
                    a[t] = a[t] - update[8 * t : 8 * t + 8, :B]
                    e[t] = e[t] - update[8 * t : 8 * t + 8, B:]
    upper = [
        jnp.concatenate([jnp.where(lane >= sub + 8 * t, a[t], 0.0) for t in range(16)], axis=0) for a in tiles
    ]
    return upper, [jnp.concatenate(e, axis=0) for e in inverse]


def dotf(a, b, dims):
    return lax.dot_general(a, b, ((dims[:1], dims[1:]), ((), ())), precision=HI, preferred_element_type=F32)


def split3(x):
    hi = x.astype(BF16)
    rest = x - hi.astype(F32)
    mid = rest.astype(BF16)
    return hi, mid, (rest - mid.astype(F32)).astype(BF16)


def row_dot(a, b, dims):
    hi, mid, low = split3(a)
    dot = lambda x, y: lax.dot_general(x, y, ((dims[:1], dims[1:]), ((), ())), preferred_element_type=F32)
    rows = [t.astype(F32) for t in (hi, mid, low)]
    one = dot(jnp.concatenate(rows, axis=0).astype(BF16), b[0])
    two = dot(jnp.concatenate(rows[:2], axis=0).astype(BF16), b[1])
    three = dot(hi, b[2])
    return (one[16:] + two[8:16] + three) + (one[8:16] + two[:8]) + one[:8]


def solve_kernel(x_ref, step_ref, wh_ref, wl_ref, d_ref, c_ref, now):
    scale = 1.0 / (8192 * 128)
    block = lambda i: x_ref[i * B : (i + 1) * B, :] * scale
    g11, g12, g22, n11, n12, n22 = (block(i) for i in range(6))
    (u_g, u_n), (e_g, e_n) = factor_blocks([g11, n11])
    u12_g = dotf(e_g, g12, (1, 0))
    u12_n = dotf(e_n, n12, (1, 0))
    s_g = g22 - dotf(u12_g, u12_g, (0, 0))
    s_n = n22 - dotf(u12_n, u12_n, (0, 0))
    (v_g, v_n), (h_g, h_n) = factor_blocks([s_g, s_n])
    low_g = -dotf(h_g, dotf(u12_g, e_g, (0, 0)), (1, 0))
    low_n = -dotf(h_n, dotf(u12_n, e_n, (0, 0)), (1, 0))
    zero = jnp.zeros((B, B), F32)
    weight = jnp.concatenate(
        [jnp.concatenate([e_g.T, low_g.T], axis=1), jnp.concatenate([zero, h_g.T], axis=1)], axis=0
    )
    hi, lo = split(weight)
    wh_ref[...] = hi
    wl_ref[...] = lo
    inv_n = jnp.concatenate(
        [jnp.concatenate([e_n, zero], axis=1), jnp.concatenate([low_n, h_n], axis=1)], axis=0
    )
    upper = jnp.concatenate(
        [jnp.concatenate([u_g, u12_g], axis=1), jnp.concatenate([zero, v_g], axis=1)], axis=0
    )
    project = jnp.concatenate(
        [jnp.concatenate([block(6), block(7)], axis=1), jnp.concatenate([block(8), block(9)], axis=1)], axis=0
    )
    load = jnp.concatenate([x_ref[10 * B : 10 * B + 1, :], x_ref[10 * B + 1 : 10 * B + 2, :]], axis=1)
    stack = jnp.concatenate([project.T, jnp.broadcast_to(load * (scale * STEP), (8, N))], axis=0)
    stack = dotf(dotf(stack, inv_n, (1, 1)), inv_n, (1, 0))
    turn = stack[:N]
    shift = stack[N:]
    index = step_ref[...]
    lane = lax.broadcasted_iota(jnp.int32, (1, N), 1)
    latest = jnp.sum(jnp.where(index == jnp.max(index, axis=1, keepdims=True), lane, 0), axis=1, keepdims=True)
    chosen = lax.broadcasted_iota(jnp.int32, (N, N), 0) == latest
    now[...] = jnp.sum(jnp.where(chosen, turn, 0.0), axis=0, keepdims=True) + shift
    d_ref[...] = jnp.zeros((8, N), F32)
    d_ref[0:1, :] = now[:1, :]
    terms = split3(turn)
    for i in range(1, STEPS):
        now[...] = row_dot(now[...], terms, (1, 0)) + shift
        d_ref[i : i + 1, :] = now[:1, :]
    c_ref[...] = row_dot(d_ref[...], split3(upper), (1, 1))[:STEPS, :]


def reduced(total, step_index):
    return pl.pallas_call(
        solve_kernel,
        out_shape=[
            jax.ShapeDtypeStruct((N, N), BF16),
            jax.ShapeDtypeStruct((N, N), BF16),
            jax.ShapeDtypeStruct((8, N), F32),
            jax.ShapeDtypeStruct((STEPS, N), F32),
        ],
        in_specs=[pl.BlockSpec(memory_space=pltpu.VMEM)] * 2,
        out_specs=[pl.BlockSpec(memory_space=pltpu.VMEM)] * 4,
        scratch_shapes=[pltpu.VMEM((8, N), F32)],
        compiler_params=pltpu.CompilerParams(vmem_limit_bytes=24 << 20),
        name="reduced",
    )(total, step_index.reshape(1, N))


def final_kernel(ch_ref, cl_ref, y_ref, f_ref, wh_ref, wl_ref, d_ref, basis_ref, res_ref, acc):
    step = pl.program_id(0)
    groups = CHUNK // B
    here = pl.ds(step * groups, groups)
    hi = ch_ref[here].reshape(CHUNK, N)
    lo = cl_ref[here].reshape(CHUNK, N)
    wh = wh_ref[...]
    out = jnp.dot(hi, wh, preferred_element_type=F32)
    out += jnp.dot(lo, wh, preferred_element_type=F32)
    out += jnp.dot(hi, wl_ref[...], preferred_element_type=F32)
    basis_ref[...] = out
    last = d_ref[2:3, :]
    before = d_ref[1:2, :]
    lane = lax.broadcasted_iota(jnp.int32, (B, B), 1)
    for g in range(CHUNK // B):
        own = pl.ds(pl.multiple_of(step * CHUNK + g * B, B), B)
        s = ch_ref[step * groups + g].astype(F32) + cl_ref[step * groups + g].astype(F32)
        z = y_ref[own, :] * last - s * before
        z = jnp.sum(z[:, :B] + z[:, B:], axis=1, keepdims=True)
        acc[...] = jnp.where(lane == g, z, acc[...])
    res_ref[...] = acc[...].T[: CHUNK // B, :] - STEP * f_ref[...]


def final(cand_h, cand_l, y, forcing, wh, wl, d):
    rows = y.shape[0]
    whole = lambda i: (0, 0)
    return pl.pallas_call(
        final_kernel,
        grid=(rows // CHUNK,),
        in_specs=[pl.BlockSpec(memory_space=pltpu.VMEM)] * 3
        + [
            pl.BlockSpec((CHUNK // B, B), lambda i: (i, 0)),
            pl.BlockSpec((N, N), whole),
            pl.BlockSpec((N, N), whole),
            pl.BlockSpec((8, N), whole),
        ],
        out_specs=[
            pl.BlockSpec((CHUNK, N), lambda i: (i, 0)),
            pl.BlockSpec((CHUNK // B, B), lambda i: (i, 0)),
        ],
        out_shape=[
            jax.ShapeDtypeStruct((rows, N), F32),
            jax.ShapeDtypeStruct((rows // B, B), F32),
        ],
        scratch_shapes=[pltpu.VMEM((B, B), F32)],
        compiler_params=pltpu.CompilerParams(vmem_limit_bytes=28 << 20),
        cost_estimate=pl.CostEstimate(flops=6 * rows * N * N, bytes_accessed=12 * rows * N, transcendentals=0),
        name="final",
    )(cand_h, cand_l, y, forcing, wh, wl, d)


def shards(snapshots, tangent, pattern, forcing, step_index):
    rows = snapshots.shape[0]
    blocks = rows // B
    codes = pattern.T
    source = codes // blocks
    block = codes % blocks
    tail_side = (source == 1) | (source == 3)
    index_map = jnp.where(
        source == 0, block, blocks + HALO * (source - 1) + block - jnp.where(tail_side, blocks - HALO, 0)
    )
    cand_h, cand_l, gram_local = front(snapshots)
    force = forcing.reshape(blocks, B)
    y, total = image(index_map, tangent, force, gram_local, cand_h, cand_l)
    wh, wl, d, coefficients = reduced(total, step_index)
    basis, residual = final(cand_h, cand_l, y, force, wh, wl, d)
    return basis, coefficients, residual.reshape(rows)


def solution(mesh):
    both = ("rows", "zone")
    in_specs = (P(both, None), P(both, None), P(both, None), P(both), P())
    out_specs = (P(both, None), P(), P(both))
    return jax.shard_map(shards, mesh=mesh, in_specs=in_specs, out_specs=out_specs, check_vma=False)
```

```python
import functools

import jax
import jax.numpy as jnp
from jax import lax
from jax.experimental import pallas as pl
from jax.experimental.pallas import tpu as pltpu
from jax.sharding import PartitionSpec as P

HALO = 4
STEPS = 3
STEP = 0.25
B = 128
N = 256
CHUNK = 1024
PACK = 1344
F32 = jnp.float32
BF16 = jnp.bfloat16
HI = lax.Precision.HIGHEST
MESH = pl.DeviceIdType.MESH


def split(x):
    hi = x.astype(BF16)
    return hi, (x - hi.astype(F32)).astype(BF16)


def tdot(a, b):
    return lax.dot_general(a, b, (((0,), (0,)), ((), ())), preferred_element_type=F32)


def front_kernel(s_hbm, ch_ref, cl_ref, g_ref, sbuf, halo, load_sem, send_sem, recv_sem):
    rows = s_hbm.shape[0]
    edge = HALO * B
    chunks = rows // CHUNK
    ring, belt = lax.axis_size("rows"), lax.axis_size("zone")
    row_id, zone_id = lax.axis_index("rows"), lax.axis_index("zone")
    loads = []
    for i in range(chunks):
        part = pl.ds(i * CHUNK, CHUNK)
        loads.append(pltpu.make_async_copy(s_hbm.at[part], sbuf.at[part], load_sem.at[i]))
        loads[-1].start()
    peers = (
        ((row_id + 1) % ring, zone_id),
        ((row_id + ring - 1) % ring, zone_id),
        (row_id, (zone_id + 1) % belt),
        (row_id, (zone_id + belt - 1) % belt),
    )
    barrier = pltpu.get_barrier_semaphore()
    for peer in peers:
        pl.semaphore_signal(barrier, inc=1, device_id=peer, device_id_type=MESH)
    pl.semaphore_wait(barrier, 4)
    copies = []
    for i, peer in enumerate(peers):
        start = rows - edge if i % 2 == 0 else 0
        copies.append(
            pltpu.make_async_remote_copy(
                src_ref=s_hbm.at[pl.ds(start, edge)], dst_ref=halo.at[i],
                send_sem=send_sem.at[i], recv_sem=recv_sem.at[i], device_id=peer, device_id_type=MESH,
            )
        )
        copies[-1].start()
    total = jnp.zeros((2 * N, N), F32)
    for i in range(chunks):
        loads[i].wait()
        part = pl.ds(i * CHUNK, CHUNK)
        hi, lo = split(sbuf[part, :])
        spot = pl.ds(i * CHUNK // B, CHUNK // B)
        ch_ref[spot] = hi.reshape(CHUNK // B, B, N)
        cl_ref[spot] = lo.reshape(CHUNK // B, B, N)
        total += tdot(jnp.concatenate([hi, lo], axis=1), hi)
    half = total[:N] * 0.5 + total[N:]
    g_ref[...] = half + half.T
    there = (True, True, zone_id > 0, zone_id < belt - 1)
    for i in (2, 3, 0, 1):
        copies[i].wait_recv()
        value = halo[i]
        if i >= 2:
            value = jnp.where(there[i], value, 0.0)
        hi, lo = split(value)
        spot = pl.ds(rows // B + i * HALO, HALO)
        ch_ref[spot] = hi.reshape(HALO, B, N)
        cl_ref[spot] = lo.reshape(HALO, B, N)
    for copy in copies:
        copy.wait_send()


def front(snapshots):
    rows = snapshots.shape[0]
    edge = HALO * B
    return pl.pallas_call(
        front_kernel,
        in_specs=[pl.BlockSpec(memory_space=pl.ANY)],
        out_specs=[pl.BlockSpec(memory_space=pltpu.VMEM)] * 3,
        out_shape=[
            jax.ShapeDtypeStruct((rows // B + 4 * HALO, B, N), BF16),
            jax.ShapeDtypeStruct((rows // B + 4 * HALO, B, N), BF16),
            jax.ShapeDtypeStruct((N, N), F32),
        ],
        scratch_shapes=[
            pltpu.VMEM((rows, N), F32),
            pltpu.VMEM((4, edge, N), F32),
            pltpu.SemaphoreType.DMA((rows // CHUNK,)),
            pltpu.SemaphoreType.DMA((4,)),
            pltpu.SemaphoreType.DMA((4,)),
        ],
        compiler_params=pltpu.CompilerParams(collective_id=1, has_side_effects=True, vmem_limit_bytes=38 << 20),
        cost_estimate=pl.CostEstimate(flops=2 * rows * N * N, bytes_accessed=8 * rows * N, transcendentals=0),
        name="front",
    )(snapshots)


PARTS = 3
PART = PACK // PARTS
STAGE_SLOTS = (1, 3, 3, 3, 3, 1)
STAGE_BASE = tuple(PARTS * sum(STAGE_SLOTS[:i]) for i in range(6))


def reach():
    rows_id = lax.axis_index("rows")
    zone_id = lax.axis_index("zone")
    core = zone_id % 2
    place = {"x": zone_id // 2, "y": rows_id % 4, "z": rows_id // 4}
    def device(axis, shift):
        at = dict(place)
        if axis == "core":
            return (rows_id, at["x"] * 2 + (1 - core))
        at[axis] = (at[axis] + shift) % 4
        return (at["z"] * 4 + at["y"], at["x"] * 2 + core)

    return core, place, device


def greet():
    _, _, device = reach()
    barrier = pltpu.get_barrier_semaphore()
    for axis, shift in [("core", 1)] + [(a, s) for a in "xyz" for s in (1, 2, 3)]:
        pl.semaphore_signal(barrier, inc=1, device_id=device(axis, shift), device_id_type=MESH)


def reduce_all(x_ref, o_ref, acc, got0, got1, got2, got3, send_sem, recv_sem):
    core, place, device = reach()
    pl.semaphore_wait(pltpu.get_barrier_semaphore(), 10)
    live = {}

    def send(stage, part, slot, src, dst, axis, shift):
        k = STAGE_BASE[stage] + part * STAGE_SLOTS[stage] + slot
        copy = pltpu.make_async_remote_copy(
            src_ref=src, dst_ref=dst, send_sem=send_sem.at[k], recv_sem=recv_sem.at[k],
            device_id=device(axis, shift), device_id_type=MESH,
        )
        copy.start()
        live[stage, part, slot] = copy

    def arrive(stage, part):
        for slot in range(STAGE_SLOTS[stage]):
            live[stage, part, slot].wait_recv()

    orders = (("x", "y", "z"), ("y", "z", "x"), ("z", "x", "y"))
    half = PART // 2
    quarter = half // 4
    mine = core * half
    for p in range(PARTS):
        send(0, p, 0, x_ref.at[pl.ds(p * PART + (1 - core) * half, half)], got0.at[p], "core", 1)
    for p, (a, b, c) in enumerate(orders):
        arrive(0, p)
        acc[p] = x_ref[pl.ds(p * PART + mine, half), :] + got0[p]
        for o in (1, 2, 3):
            there = (place[a] + o) % 4
            send(1, p, o - 1, acc.at[p, pl.ds(there * quarter, quarter)], got1.at[p, o - 1], a, o)
    for p, (a, b, c) in enumerate(orders):
        arrive(1, p)
        slot = got2.at[p, place[b]]
        slot[...] = acc[p, pl.ds(place[a] * quarter, quarter), :] + got1[p, 0] + got1[p, 1] + got1[p, 2]
        for o in (1, 2, 3):
            send(2, p, o - 1, slot, slot, b, o)
    for p, (a, b, c) in enumerate(orders):
        arrive(2, p)
        slot = got3.at[p, place[c]]
        slot[...] = got2[p, 0] + got2[p, 1] + got2[p, 2] + got2[p, 3]
        for o in (1, 2, 3):
            send(3, p, o - 1, slot, slot, c, o)
    for p, (a, b, c) in enumerate(orders):
        arrive(3, p)
        spot = o_ref.at[pl.ds(p * PART + mine + place[a] * quarter, quarter)]
        spot[...] = got3[p, 0] + got3[p, 1] + got3[p, 2] + got3[p, 3]
        for o in (1, 2, 3):
            send(4, p, o - 1, spot, spot, a, o)
    for p in range(PARTS):
        arrive(4, p)
        spot = o_ref.at[pl.ds(p * PART + mine, half)]
        send(5, p, 0, spot, spot, "core", 1)
    for p in range(PARTS):
        arrive(5, p)
    for copy in live.values():
        copy.wait_send()


def decode(code, blocks):
    source = code // blocks
    block = code % blocks
    tail = jnp.where((source == 1) | (source == 3), blocks - HALO, 0)
    return jnp.where(source == 0, block, blocks + HALO * (source - 1) + block - tail)


def image_kernel(
    code_ref, t_ref, f_ref, g_ref, cand_h, cand_l, y_ref, total_ref,
    ybuf_h, ybuf_l, acc, load_acc, pack_ref, *exchange,
):
    step = pl.program_id(0)

    @pl.when(step == 0)
    def _():
        greet()
        acc[...] = jnp.zeros_like(acc)
        load_acc[...] = jnp.zeros_like(load_acc)

    groups = CHUNK // B
    force = f_ref[...].T
    total = jnp.zeros((8, N), F32)
    for g in range(groups):
        picks = [decode(code_ref[e, step * groups + g], cand_h.shape[0] - 4 * HALO) for e in range(4)]
        tiles = t_ref[g * B : (g + 1) * B, :]
        image = jnp.dot(tiles, jnp.concatenate([cand_h[p] for p in picks], axis=0), preferred_element_type=F32)
        image += jnp.dot(tiles, jnp.concatenate([cand_l[p] for p in picks], axis=0), preferred_element_type=F32)
        own = pl.ds(pl.multiple_of(step * CHUNK + g * B, B), B)
        y = cand_h[step * groups + g].astype(F32) + cand_l[step * groups + g].astype(F32) + STEP * image
        y_ref[own, :] = y
        hi, lo = split(y)
        ybuf_h[g * B : (g + 1) * B, :] = hi
        ybuf_l[g * B : (g + 1) * B, :] = lo
        total += jnp.sum((y * force[:, g : g + 1]).reshape(B // 8, 8, N), axis=0)
    load_acc[...] += total
    here = pl.ds(step * groups, groups)
    yh = ybuf_h[...]
    yl = ybuf_l[...]
    one = tdot(jnp.concatenate([yh, yl], axis=1), cand_h[here].reshape(CHUNK, N))
    acc[0] += one[:N] + one[N:]
    two = tdot(jnp.concatenate([yh, yl, cand_l[here].reshape(CHUNK, N)], axis=1), yh)
    acc[1] += two[:N] * 0.5 + two[N : 2 * N]
    acc[2] += two[2 * N :]

    @pl.when(step == pl.num_programs(0) - 1)
    def _():
        normal = acc[1] + acc[1].T
        project = acc[0] + acc[2].T
        gram_matrix = g_ref[...]
        blocks = []
        for matrix in (gram_matrix, normal):
            blocks += [matrix[:B, :B], matrix[:B, B:], matrix[B:, B:]]
        blocks += [project[:B, :B], project[:B, B:], project[B:, :B], project[B:, B:]]
        for i, block in enumerate(blocks):
            pack_ref[i * B : (i + 1) * B, :] = block
        load = jnp.sum(load_acc[...], axis=0, keepdims=True)
        pack_ref[10 * B :, :] = jnp.zeros((PACK - 10 * B, B), F32)
        pack_ref[10 * B : 10 * B + 1, :] = load[:, :B]
        pack_ref[10 * B + 1 : 10 * B + 2, :] = load[:, B:]
        reduce_all(pack_ref, *exchange)
        total_ref[...] = exchange[0][...]


def image(codes, tangent, forcing, gram_local, cand_h, cand_l):
    rows = tangent.shape[0]
    half = PART // 2
    count = PARTS * sum(STAGE_SLOTS)
    return pl.pallas_call(
        image_kernel,
        grid_spec=pltpu.PrefetchScalarGridSpec(
            num_scalar_prefetch=1,
            grid=(rows // CHUNK,),
            in_specs=[
                pl.BlockSpec((CHUNK, 4 * B), lambda i, *_: (i, 0)),
                pl.BlockSpec((CHUNK // B, B), lambda i, *_: (i, 0)),
                pl.BlockSpec(memory_space=pltpu.VMEM),
                pl.BlockSpec(memory_space=pltpu.VMEM),
                pl.BlockSpec(memory_space=pltpu.VMEM),
            ],
            out_specs=[
                pl.BlockSpec(memory_space=pltpu.VMEM),
                pl.BlockSpec(memory_space=pltpu.VMEM),
            ],
            scratch_shapes=[
                pltpu.VMEM((CHUNK, N), BF16),
                pltpu.VMEM((CHUNK, N), BF16),
                pltpu.VMEM((3, N, N), F32),
                pltpu.VMEM((8, N), F32),
                pltpu.VMEM((PACK, B), F32),
                pltpu.VMEM((PACK, B), F32),
                pltpu.VMEM((PARTS, half, B), F32),
                pltpu.VMEM((PARTS, half, B), F32),
                pltpu.VMEM((PARTS, 3, half // 4, B), F32),
                pltpu.VMEM((PARTS, 4, half // 4, B), F32),
                pltpu.VMEM((PARTS, 4, half // 4, B), F32),
                pltpu.SemaphoreType.DMA((count,)),
                pltpu.SemaphoreType.DMA((count,)),
            ],
        ),
        out_shape=[
            jax.ShapeDtypeStruct((rows, N), F32),
            jax.ShapeDtypeStruct((PACK, B), F32),
        ],
        compiler_params=pltpu.CompilerParams(collective_id=0, has_side_effects=True, vmem_limit_bytes=28 << 20),
        cost_estimate=pl.CostEstimate(flops=20 * rows * N * N, bytes_accessed=8 * rows * N, transcendentals=0),
        name="image",
    )(codes, tangent, forcing, gram_local, cand_h, cand_l)


def split3f(x):
    hi = x.astype(BF16).astype(F32)
    mid = (x - hi).astype(BF16).astype(F32)
    return hi, mid, (x - hi - mid)


def factor_blocks(matrices):
    tiles = [[m[8 * t : 8 * t + 8, :] for t in range(16)] for m in matrices]
    lane = lax.broadcasted_iota(jnp.int32, (8, B), 1)
    sub = lax.broadcasted_iota(jnp.int32, (8, B), 0)
    inverse = [[(lane == sub + 8 * t).astype(F32) for t in range(16)] for _ in matrices]
    for p in range(16):
        for a, e in zip(tiles, inverse):
            spread = lambda t: [jnp.broadcast_to(a[t][:, 8 * p + c : 8 * p + c + 1], (8, B)) for c in range(8)]
            column = spread(p)
            pivot, link = [], {}
            for k in range(8):
                pivot.append(lax.rsqrt(column[k][k : k + 1, :]))
                column[k] = column[k] * pivot[k]
                for c in range(k + 1, 8):
                    link[k, c] = column[k][c : c + 1, :]
                    column[c] = column[c] - column[k] * link[k, c]
            rows, erows = [], []
            own, eown = a[p], e[p]
            for k in range(8):
                rows.append(own[k : k + 1, :] * pivot[k])
                erows.append(eown[k : k + 1, :] * pivot[k])
                own = own - column[k] * rows[k]
                eown = eown - column[k] * erows[k]
            if p + 1 < 16:
                t = p + 1
                column = spread(t)
                for k in range(8):
                    column[k] = column[k] * pivot[k]
                    for c in range(k + 1, 8):
                        column[c] = column[c] - column[k] * link[k, c]
                    a[t] = a[t] - column[k] * rows[k]
                    e[t] = e[t] - column[k] * erows[k]
            a[p] = jnp.concatenate(rows, axis=0)
            e[p] = jnp.concatenate(erows, axis=0)
            if p + 2 < 16:
                ah, am, al = split3f(a[p])
                eh, em, el = split3f(e[p])
                lhs = jnp.concatenate([ah, ah, am, ah, al, am], axis=0).astype(BF16)
                rhs = jnp.concatenate(
                    [jnp.concatenate([ah, am, ah, al, ah, am], axis=0), jnp.concatenate([eh, em, eh, el, eh, em], axis=0)], axis=1
                ).astype(BF16)
                update = tdot(lhs, rhs)
                for t in range(p + 2, 16):
                    a[t] = a[t] - update[8 * t : 8 * t + 8, :B]
                    e[t] = e[t] - update[8 * t : 8 * t + 8, B:]
    upper = [
        jnp.concatenate([jnp.where(lane >= sub + 8 * t, a[t], 0.0) for t in range(16)], axis=0) for a in tiles
    ]
    return upper, [jnp.concatenate(e, axis=0) for e in inverse]


def dotf(a, b, dims):
    return lax.dot_general(a, b, ((dims[:1], dims[1:]), ((), ())), precision=HI, preferred_element_type=F32)


def split3(x):
    hi = x.astype(BF16)
    rest = x - hi.astype(F32)
    mid = rest.astype(BF16)
    return hi, mid, (rest - mid.astype(F32)).astype(BF16)


def row_dot(a, b, dims):
    hi, mid, low = split3(a)
    dot = lambda x, y: lax.dot_general(x, y, ((dims[:1], dims[1:]), ((), ())), preferred_element_type=F32)
    rows = [t.astype(F32) for t in (hi, mid, low)]
    one = dot(jnp.concatenate(rows, axis=0).astype(BF16), b[0])
    two = dot(jnp.concatenate(rows[:2], axis=0).astype(BF16), b[1])
    three = dot(hi, b[2])
    return (one[16:] + two[8:16] + three) + (one[8:16] + two[:8]) + one[:8]


def factor_step(x_ref, weight, inverse, stack, upper):
    scale = 1.0 / (8192 * 128)
    block = lambda i: x_ref[i * B : (i + 1) * B, :] * scale
    g11, g12, g22, n11, n12, n22 = (block(i) for i in range(6))
    (u_g, u_n), (e_g, e_n) = factor_blocks([g11, n11])
    u12_g = dotf(e_g, g12, (1, 0))
    u12_n = dotf(e_n, n12, (1, 0))
    s_g = g22 - dotf(u12_g, u12_g, (0, 0))
    s_n = n22 - dotf(u12_n, u12_n, (0, 0))
    (v_g, v_n), (h_g, h_n) = factor_blocks([s_g, s_n])
    low_g = -dotf(h_g, dotf(u12_g, e_g, (0, 0)), (1, 0))
    low_n = -dotf(h_n, dotf(u12_n, e_n, (0, 0)), (1, 0))
    zero = jnp.zeros((B, B), F32)
    hi, lo = split(
        jnp.concatenate(
            [jnp.concatenate([e_g.T, low_g.T], axis=1), jnp.concatenate([zero, h_g.T], axis=1)], axis=0
        )
    )
    weight[:N, :] = hi
    weight[N : 2 * N, :] = hi
    weight[2 * N :, :] = lo
    inverse[...] = jnp.concatenate(
        [jnp.concatenate([e_n, zero], axis=1), jnp.concatenate([low_n, h_n], axis=1)], axis=0
    )
    upper[...] = jnp.concatenate(
        [jnp.concatenate([u_g, u12_g], axis=1), jnp.concatenate([zero, v_g], axis=1)], axis=0
    )
    project = jnp.concatenate(
        [jnp.concatenate([block(6), block(7)], axis=1), jnp.concatenate([block(8), block(9)], axis=1)], axis=0
    )
    load = jnp.concatenate([x_ref[10 * B : 10 * B + 1, :], x_ref[10 * B + 1 : 10 * B + 2, :]], axis=1)
    stack[:N, :] = project.T
    stack[N:, :] = jnp.broadcast_to(load * (scale * STEP), (8, N))


def finish_kernel(
    x_ref, step_ref, f_ref, ch_ref, cl_ref, y_ref, basis_ref, c_ref, res_ref,
    weight, inverse, stack, upper, now, states,
):
    step = pl.program_id(0)
    groups = CHUNK // B

    def basis():
        here = pl.ds((step - 1) * groups, groups)
        hi = ch_ref[here].reshape(CHUNK, N)
        lo = cl_ref[here].reshape(CHUNK, N)
        basis_ref[...] = jnp.dot(jnp.concatenate([hi, lo, hi], axis=1), weight[...], preferred_element_type=F32)

    def half_turn():
        stack[...] = dotf(stack[...], inverse[...], (1, 1))

    def turn():
        stack[...] = dotf(stack[...], inverse[...], (1, 0))
        index = step_ref[...]
        lane = lax.broadcasted_iota(jnp.int32, (1, N), 1)
        latest = jnp.sum(jnp.where(index == jnp.max(index, axis=1, keepdims=True), lane, 0), axis=1, keepdims=True)
        chosen = lax.broadcasted_iota(jnp.int32, (N, N), 0) == latest
        now[...] = jnp.sum(jnp.where(chosen, stack[:N, :], 0.0), axis=0, keepdims=True) + stack[N:, :]
        states[...] = jnp.zeros((8, N), F32)
        states[0:1, :] = now[:1, :]

    def advance(i):
        now[...] = row_dot(now[...], split3(stack[:N, :]), (1, 0)) + stack[N:, :]
        states[i : i + 1, :] = now[:1, :]

    def coefficients():
        c_ref[...] = row_dot(states[...], split3(upper[...]), (1, 1))[:STEPS, :]

    def residual(*chunks):
        last = states[2:3, :]
        before = states[1:2, :]
        lane = lax.broadcasted_iota(jnp.int32, (B, B), 1)
        for chunk in chunks:
            columns = jnp.zeros((B, B), F32)
            for g in range(groups):
                at = chunk * groups + g
                s = ch_ref[at].astype(F32) + cl_ref[at].astype(F32)
                z = y_ref[at * B : (at + 1) * B, :] * last - s * before
                z = jnp.sum(z[:, :B] + z[:, B:], axis=1, keepdims=True)
                columns = jnp.where(lane == g, z, columns)
            rows = slice(chunk * groups, (chunk + 1) * groups)
            res_ref[rows, :] = columns.T[:groups, :] - STEP * f_ref[rows, :]

    def last_piece(k):
        if k == 5:
            coefficients()
        residual(2 * (k - 5), 2 * (k - 5) + 1)

    pieces = [half_turn, turn, functools.partial(advance, 1), functools.partial(advance, 2)]
    pieces += [functools.partial(last_piece, k) for k in (5, 6, 7, 8)]

    @pl.when(step == 0)
    def _():
        factor_step(x_ref, weight, inverse, stack, upper)

    for k, piece in enumerate(pieces):

        @pl.when(step == k + 1)
        def _(piece=piece):
            basis()
            piece()


def finish(total, step_index, forcing, cand_h, cand_l, y):
    rows = y.shape[0]
    whole = pl.BlockSpec(memory_space=pltpu.VMEM)
    return pl.pallas_call(
        finish_kernel,
        grid=(rows // CHUNK + 1,),
        in_specs=[whole] * 6,
        out_specs=[pl.BlockSpec((CHUNK, N), lambda i: (jnp.maximum(i - 1, 0), 0)), whole, whole],
        out_shape=[
            jax.ShapeDtypeStruct((rows, N), F32),
            jax.ShapeDtypeStruct((STEPS, N), F32),
            jax.ShapeDtypeStruct((rows // B, B), F32),
        ],
        scratch_shapes=[
            pltpu.VMEM((3 * N, N), BF16),
            pltpu.VMEM((N, N), F32),
            pltpu.VMEM((N + 8, N), F32),
            pltpu.VMEM((N, N), F32),
            pltpu.VMEM((8, N), F32),
            pltpu.VMEM((8, N), F32),
        ],
        compiler_params=pltpu.CompilerParams(vmem_limit_bytes=28 << 20),
        cost_estimate=pl.CostEstimate(flops=6 * rows * N * N, bytes_accessed=4 * rows * N, transcendentals=0),
        name="finish",
    )(total, step_index.reshape(1, N), forcing, cand_h, cand_l, y)


def shards(snapshots, tangent, pattern, forcing, step_index):
    rows = snapshots.shape[0]
    blocks = rows // B
    cand_h, cand_l, gram_local = front(snapshots)
    force = forcing.reshape(blocks, B)
    y, total = image(pattern.T, tangent, force, gram_local, cand_h, cand_l)
    basis, coefficients, residual = finish(total, step_index, force, cand_h, cand_l, y)
    return basis, coefficients, residual.reshape(rows)


def solution(mesh):
    both = ("rows", "zone")
    in_specs = (P(both, None), P(both, None), P(both, None), P(both), P())
    out_specs = (P(both, None), P(), P(both))
    return jax.shard_map(shards, mesh=mesh, in_specs=in_specs, out_specs=out_specs, check_vma=False)
```

```python
import functools

import jax
import jax.numpy as jnp
from jax import lax
from jax.experimental import pallas as pl
from jax.experimental.pallas import tpu as pltpu
from jax.sharding import PartitionSpec as P

HALO = 4
STEPS = 3
STEP = 0.25
B = 128
N = 256
CHUNK = 1024
SPAN = 2048
PACK = 1344
F32 = jnp.float32
BF16 = jnp.bfloat16
HI = lax.Precision.HIGHEST
MESH = pl.DeviceIdType.MESH


def split(x):
    hi = x.astype(BF16)
    return hi, (x - hi.astype(F32)).astype(BF16)


def tdot(a, b):
    return lax.dot_general(a, b, (((0,), (0,)), ((), ())), preferred_element_type=F32)


def front_kernel(s_hbm, ch_ref, cl_ref, g_ref, sbuf, halo, load_sem, send_sem, recv_sem):
    rows = s_hbm.shape[0]
    edge = HALO * B
    chunks = rows // CHUNK
    ring, belt = lax.axis_size("rows"), lax.axis_size("zone")
    row_id, zone_id = lax.axis_index("rows"), lax.axis_index("zone")
    loads = []
    for i in range(chunks):
        part = pl.ds(i * CHUNK, CHUNK)
        loads.append(pltpu.make_async_copy(s_hbm.at[part], sbuf.at[part], load_sem.at[i]))
        loads[-1].start()
    peers = (
        ((row_id + 1) % ring, zone_id),
        ((row_id + ring - 1) % ring, zone_id),
        (row_id, (zone_id + 1) % belt),
        (row_id, (zone_id + belt - 1) % belt),
    )
    barrier = pltpu.get_barrier_semaphore()
    for peer in peers:
        pl.semaphore_signal(barrier, inc=1, device_id=peer, device_id_type=MESH)
    pl.semaphore_wait(barrier, 4)
    copies = []
    for i, peer in enumerate(peers):
        start = rows - edge if i % 2 == 0 else 0
        copies.append(
            pltpu.make_async_remote_copy(
                src_ref=s_hbm.at[pl.ds(start, edge)], dst_ref=halo.at[i],
                send_sem=send_sem.at[i], recv_sem=recv_sem.at[i], device_id=peer, device_id_type=MESH,
            )
        )
        copies[-1].start()
    total = jnp.zeros((2 * N, N), F32)
    for i in range(chunks):
        loads[i].wait()
        part = pl.ds(i * CHUNK, CHUNK)
        hi, lo = split(sbuf[part, :])
        spot = pl.ds(i * CHUNK // B, CHUNK // B)
        ch_ref[spot] = hi.reshape(CHUNK // B, B, N)
        cl_ref[spot] = lo.reshape(CHUNK // B, B, N)
        total += tdot(jnp.concatenate([hi, lo], axis=1), hi)
    half = total[:N] * 0.5 + total[N:]
    g_ref[...] = half + half.T
    there = (True, True, zone_id > 0, zone_id < belt - 1)
    for i in (2, 3, 0, 1):
        copies[i].wait_recv()
        value = halo[i]
        if i >= 2:
            value = jnp.where(there[i], value, 0.0)
        hi, lo = split(value)
        spot = pl.ds(rows // B + i * HALO, HALO)
        ch_ref[spot] = hi.reshape(HALO, B, N)
        cl_ref[spot] = lo.reshape(HALO, B, N)
    for copy in copies:
        copy.wait_send()


def front(snapshots):
    rows = snapshots.shape[0]
    edge = HALO * B
    return pl.pallas_call(
        front_kernel,
        in_specs=[pl.BlockSpec(memory_space=pl.ANY)],
        out_specs=[pl.BlockSpec(memory_space=pltpu.VMEM)] * 3,
        out_shape=[
            jax.ShapeDtypeStruct((rows // B + 4 * HALO, B, N), BF16),
            jax.ShapeDtypeStruct((rows // B + 4 * HALO, B, N), BF16),
            jax.ShapeDtypeStruct((N, N), F32),
        ],
        scratch_shapes=[
            pltpu.VMEM((rows, N), F32),
            pltpu.VMEM((4, edge, N), F32),
            pltpu.SemaphoreType.DMA((rows // CHUNK,)),
            pltpu.SemaphoreType.DMA((4,)),
            pltpu.SemaphoreType.DMA((4,)),
        ],
        compiler_params=pltpu.CompilerParams(collective_id=1, has_side_effects=True, vmem_limit_bytes=38 << 20),
        cost_estimate=pl.CostEstimate(flops=2 * rows * N * N, bytes_accessed=8 * rows * N, transcendentals=0),
        name="front",
    )(snapshots)


PARTS = 3
PART = PACK // PARTS
STAGE_SLOTS = (1, 3, 3, 3, 3, 1)
STAGE_BASE = tuple(PARTS * sum(STAGE_SLOTS[:i]) for i in range(6))


def reach():
    rows_id = lax.axis_index("rows")
    zone_id = lax.axis_index("zone")
    core = zone_id % 2
    place = {"x": zone_id // 2, "y": rows_id % 4, "z": rows_id // 4}
    def device(axis, shift):
        at = dict(place)
        if axis == "core":
            return (rows_id, at["x"] * 2 + (1 - core))
        at[axis] = (at[axis] + shift) % 4
        return (at["z"] * 4 + at["y"], at["x"] * 2 + core)

    return core, place, device


def greet():
    _, _, device = reach()
    barrier = pltpu.get_barrier_semaphore()
    for axis, shift in [("core", 1)] + [(a, s) for a in "xyz" for s in (1, 2, 3)]:
        pl.semaphore_signal(barrier, inc=1, device_id=device(axis, shift), device_id_type=MESH)


def reduce_all(x_ref, o_ref, acc, got0, got1, got2, got3, send_sem, recv_sem):
    core, place, device = reach()
    pl.semaphore_wait(pltpu.get_barrier_semaphore(), 10)
    live = {}

    def send(stage, part, slot, src, dst, axis, shift):
        k = STAGE_BASE[stage] + part * STAGE_SLOTS[stage] + slot
        copy = pltpu.make_async_remote_copy(
            src_ref=src, dst_ref=dst, send_sem=send_sem.at[k], recv_sem=recv_sem.at[k],
            device_id=device(axis, shift), device_id_type=MESH,
        )
        copy.start()
        live[stage, part, slot] = copy

    def arrive(stage, part):
        for slot in range(STAGE_SLOTS[stage]):
            live[stage, part, slot].wait_recv()

    orders = (("x", "y", "z"), ("y", "z", "x"), ("z", "x", "y"))
    half = PART // 2
    quarter = half // 4
    mine = core * half
    for p in range(PARTS):
        send(0, p, 0, x_ref.at[pl.ds(p * PART + (1 - core) * half, half)], got0.at[p], "core", 1)
    for p, (a, b, c) in enumerate(orders):
        arrive(0, p)
        acc[p] = x_ref[pl.ds(p * PART + mine, half), :] + got0[p]
        for o in (1, 2, 3):
            there = (place[a] + o) % 4
            send(1, p, o - 1, acc.at[p, pl.ds(there * quarter, quarter)], got1.at[p, o - 1], a, o)
    for p, (a, b, c) in enumerate(orders):
        arrive(1, p)
        slot = got2.at[p, place[b]]
        slot[...] = acc[p, pl.ds(place[a] * quarter, quarter), :] + got1[p, 0] + got1[p, 1] + got1[p, 2]
        for o in (1, 2, 3):
            send(2, p, o - 1, slot, slot, b, o)
    for p, (a, b, c) in enumerate(orders):
        arrive(2, p)
        slot = got3.at[p, place[c]]
        slot[...] = got2[p, 0] + got2[p, 1] + got2[p, 2] + got2[p, 3]
        for o in (1, 2, 3):
            send(3, p, o - 1, slot, slot, c, o)
    for p, (a, b, c) in enumerate(orders):
        arrive(3, p)
        spot = o_ref.at[pl.ds(p * PART + mine + place[a] * quarter, quarter)]
        spot[...] = got3[p, 0] + got3[p, 1] + got3[p, 2] + got3[p, 3]
        for o in (1, 2, 3):
            send(4, p, o - 1, spot, spot, a, o)
    for p in range(PARTS):
        arrive(4, p)
        spot = o_ref.at[pl.ds(p * PART + mine, half)]
        send(5, p, 0, spot, spot, "core", 1)
    for p in range(PARTS):
        arrive(5, p)
    for copy in live.values():
        copy.wait_send()


def decode(code, blocks):
    source = code // blocks
    block = code % blocks
    tail = jnp.where((source == 1) | (source == 3), blocks - HALO, 0)
    return jnp.where(source == 0, block, blocks + HALO * (source - 1) + block - tail)


def image_kernel(
    code_ref, t_ref, f_ref, g_ref, cand_h, cand_l, y_ref, total_ref,
    ybuf_h, ybuf_l, acc, load_acc, pack_ref, *exchange,
):
    step = pl.program_id(0)

    @pl.when(step == 0)
    def _():
        greet()
        acc[...] = jnp.zeros_like(acc)
        load_acc[...] = jnp.zeros_like(load_acc)

    groups = CHUNK // B
    force = f_ref[...].T
    total = jnp.zeros((8, N), F32)
    for g in range(groups):
        picks = [decode(code_ref[e, step * groups + g], cand_h.shape[0] - 4 * HALO) for e in range(4)]
        tiles = t_ref[g * B : (g + 1) * B, :]
        image = jnp.dot(tiles, jnp.concatenate([cand_h[p] for p in picks], axis=0), preferred_element_type=F32)
        image += jnp.dot(tiles, jnp.concatenate([cand_l[p] for p in picks], axis=0), preferred_element_type=F32)
        own = pl.ds(pl.multiple_of(step * CHUNK + g * B, B), B)
        y = cand_h[step * groups + g].astype(F32) + cand_l[step * groups + g].astype(F32) + STEP * image
        y_ref[own, :] = y
        hi, lo = split(y)
        ybuf_h[g * B : (g + 1) * B, :] = hi
        ybuf_l[g * B : (g + 1) * B, :] = lo
        total += jnp.sum((y * force[:, g : g + 1]).reshape(B // 8, 8, N), axis=0)
    load_acc[...] += total
    here = pl.ds(step * groups, groups)
    yh = ybuf_h[...]
    yl = ybuf_l[...]
    one = tdot(jnp.concatenate([yh, yl], axis=1), cand_h[here].reshape(CHUNK, N))
    acc[0] += one[:N] + one[N:]
    two = tdot(jnp.concatenate([yh, yl, cand_l[here].reshape(CHUNK, N)], axis=1), yh)
    acc[1] += two[:N] * 0.5 + two[N : 2 * N]
    acc[2] += two[2 * N :]

    @pl.when(step == pl.num_programs(0) - 1)
    def _():
        normal = acc[1] + acc[1].T
        project = acc[0] + acc[2].T
        gram_matrix = g_ref[...]
        blocks = []
        for matrix in (gram_matrix, normal):
            blocks += [matrix[:B, :B], matrix[:B, B:], matrix[B:, B:]]
        blocks += [project[:B, :B], project[:B, B:], project[B:, :B], project[B:, B:]]
        for i, block in enumerate(blocks):
            pack_ref[i * B : (i + 1) * B, :] = block
        load = jnp.sum(load_acc[...], axis=0, keepdims=True)
        pack_ref[10 * B :, :] = jnp.zeros((PACK - 10 * B, B), F32)
        pack_ref[10 * B : 10 * B + 1, :] = load[:, :B]
        pack_ref[10 * B + 1 : 10 * B + 2, :] = load[:, B:]
        reduce_all(pack_ref, *exchange)
        total_ref[...] = exchange[0][...]


def image(codes, tangent, forcing, gram_local, cand_h, cand_l):
    rows = tangent.shape[0]
    half = PART // 2
    count = PARTS * sum(STAGE_SLOTS)
    return pl.pallas_call(
        image_kernel,
        grid_spec=pltpu.PrefetchScalarGridSpec(
            num_scalar_prefetch=1,
            grid=(rows // CHUNK,),
            in_specs=[
                pl.BlockSpec((CHUNK, 4 * B), lambda i, *_: (i, 0)),
                pl.BlockSpec((CHUNK // B, B), lambda i, *_: (i, 0)),
                pl.BlockSpec(memory_space=pltpu.VMEM),
                pl.BlockSpec(memory_space=pltpu.VMEM),
                pl.BlockSpec(memory_space=pltpu.VMEM),
            ],
            out_specs=[
                pl.BlockSpec(memory_space=pltpu.VMEM),
                pl.BlockSpec(memory_space=pltpu.VMEM),
            ],
            scratch_shapes=[
                pltpu.VMEM((CHUNK, N), BF16),
                pltpu.VMEM((CHUNK, N), BF16),
                pltpu.VMEM((3, N, N), F32),
                pltpu.VMEM((8, N), F32),
                pltpu.VMEM((PACK, B), F32),
                pltpu.VMEM((PACK, B), F32),
                pltpu.VMEM((PARTS, half, B), F32),
                pltpu.VMEM((PARTS, half, B), F32),
                pltpu.VMEM((PARTS, 3, half // 4, B), F32),
                pltpu.VMEM((PARTS, 4, half // 4, B), F32),
                pltpu.VMEM((PARTS, 4, half // 4, B), F32),
                pltpu.SemaphoreType.DMA((count,)),
                pltpu.SemaphoreType.DMA((count,)),
            ],
        ),
        out_shape=[
            jax.ShapeDtypeStruct((rows, N), F32),
            jax.ShapeDtypeStruct((PACK, B), F32),
        ],
        compiler_params=pltpu.CompilerParams(collective_id=0, has_side_effects=True, vmem_limit_bytes=28 << 20),
        cost_estimate=pl.CostEstimate(flops=20 * rows * N * N, bytes_accessed=8 * rows * N, transcendentals=0),
        name="image",
    )(codes, tangent, forcing, gram_local, cand_h, cand_l)


def split3f(x):
    hi = x.astype(BF16).astype(F32)
    mid = (x - hi).astype(BF16).astype(F32)
    return hi, mid, (x - hi - mid)


def factor_blocks(matrices):
    tiles = [[m[8 * t : 8 * t + 8, :] for t in range(16)] for m in matrices]
    lane = lax.broadcasted_iota(jnp.int32, (8, B), 1)
    sub = lax.broadcasted_iota(jnp.int32, (8, B), 0)
    inverse = [[(lane == sub + 8 * t).astype(F32) for t in range(16)] for _ in matrices]
    for p in range(16):
        for a, e in zip(tiles, inverse):
            spread = lambda t: [jnp.broadcast_to(a[t][:, 8 * p + c : 8 * p + c + 1], (8, B)) for c in range(8)]
            column = spread(p)
            pivot, link = [], {}
            for k in range(8):
                pivot.append(lax.rsqrt(column[k][k : k + 1, :]))
                column[k] = column[k] * pivot[k]
                for c in range(k + 1, 8):
                    link[k, c] = column[k][c : c + 1, :]
                    column[c] = column[c] - column[k] * link[k, c]
            rows, erows = [], []
            own, eown = a[p], e[p]
            for k in range(8):
                rows.append(own[k : k + 1, :] * pivot[k])
                erows.append(eown[k : k + 1, :] * pivot[k])
                own = own - column[k] * rows[k]
                eown = eown - column[k] * erows[k]
            if p + 1 < 16:
                t = p + 1
                column = spread(t)
                for k in range(8):
                    column[k] = column[k] * pivot[k]
                    for c in range(k + 1, 8):
                        column[c] = column[c] - column[k] * link[k, c]
                    a[t] = a[t] - column[k] * rows[k]
                    e[t] = e[t] - column[k] * erows[k]
            a[p] = jnp.concatenate(rows, axis=0)
            e[p] = jnp.concatenate(erows, axis=0)
            if p + 2 < 16:
                ah, am, al = split3f(a[p])
                eh, em, el = split3f(e[p])
                lhs = jnp.concatenate([ah, ah, am, ah, al, am], axis=0).astype(BF16)
                rhs = jnp.concatenate(
                    [jnp.concatenate([ah, am, ah, al, ah, am], axis=0), jnp.concatenate([eh, em, eh, el, eh, em], axis=0)], axis=1
                ).astype(BF16)
                update = tdot(lhs, rhs)
                for t in range(p + 2, 16):
                    a[t] = a[t] - update[8 * t : 8 * t + 8, :B]
                    e[t] = e[t] - update[8 * t : 8 * t + 8, B:]
    upper = [
        jnp.concatenate([jnp.where(lane >= sub + 8 * t, a[t], 0.0) for t in range(16)], axis=0) for a in tiles
    ]
    return upper, [jnp.concatenate(e, axis=0) for e in inverse]


def dotf(a, b, dims):
    return lax.dot_general(a, b, ((dims[:1], dims[1:]), ((), ())), precision=HI, preferred_element_type=F32)


def split3(x):
    hi = x.astype(BF16)
    rest = x - hi.astype(F32)
    mid = rest.astype(BF16)
    return hi, mid, (rest - mid.astype(F32)).astype(BF16)


def row_dot(a, b, dims):
    hi, mid, low = split3(a)
    dot = lambda x, y: lax.dot_general(x, y, ((dims[:1], dims[1:]), ((), ())), preferred_element_type=F32)
    rows = [t.astype(F32) for t in (hi, mid, low)]
    one = dot(jnp.concatenate(rows, axis=0).astype(BF16), b[0])
    two = dot(jnp.concatenate(rows[:2], axis=0).astype(BF16), b[1])
    three = dot(hi, b[2])
    return (one[16:] + two[8:16] + three) + (one[8:16] + two[:8]) + one[:8]


def factor_step(x_ref, weight, inverse, stack, upper):
    scale = 1.0 / (8192 * 128)
    block = lambda i: x_ref[i * B : (i + 1) * B, :] * scale
    g11, g12, g22, n11, n12, n22 = (block(i) for i in range(6))
    (u_g, u_n), (e_g, e_n) = factor_blocks([g11, n11])
    u12_g = dotf(e_g, g12, (1, 0))
    u12_n = dotf(e_n, n12, (1, 0))
    s_g = g22 - dotf(u12_g, u12_g, (0, 0))
    s_n = n22 - dotf(u12_n, u12_n, (0, 0))
    (v_g, v_n), (h_g, h_n) = factor_blocks([s_g, s_n])
    low_g = -dotf(h_g, dotf(u12_g, e_g, (0, 0)), (1, 0))
    low_n = -dotf(h_n, dotf(u12_n, e_n, (0, 0)), (1, 0))
    zero = jnp.zeros((B, B), F32)
    hi, lo = split(
        jnp.concatenate(
            [jnp.concatenate([e_g.T, low_g.T], axis=1), jnp.concatenate([zero, h_g.T], axis=1)], axis=0
        )
    )
    weight[:N, :] = hi
    weight[N : 2 * N, :] = hi
    weight[2 * N :, :] = lo
    inverse[...] = jnp.concatenate(
        [jnp.concatenate([e_n, zero], axis=1), jnp.concatenate([low_n, h_n], axis=1)], axis=0
    )
    upper[...] = jnp.concatenate(
        [jnp.concatenate([u_g, u12_g], axis=1), jnp.concatenate([zero, v_g], axis=1)], axis=0
    )
    project = jnp.concatenate(
        [jnp.concatenate([block(6), block(7)], axis=1), jnp.concatenate([block(8), block(9)], axis=1)], axis=0
    )
    load = jnp.concatenate([x_ref[10 * B : 10 * B + 1, :], x_ref[10 * B + 1 : 10 * B + 2, :]], axis=1)
    stack[:N, :] = project.T
    stack[N:, :] = jnp.broadcast_to(load * (scale * STEP), (8, N))


def finish_kernel(
    x_ref, step_ref, f_ref, ch_ref, cl_ref, y_ref, basis_ref, c_ref, res_ref,
    weight, inverse, stack, upper, now, states,
):
    step = pl.program_id(0)
    groups = CHUNK // B

    def basis():
        here = pl.ds((step - 1) * (SPAN // B), SPAN // B)
        hi = ch_ref[here].reshape(SPAN, N)
        lo = cl_ref[here].reshape(SPAN, N)
        basis_ref[...] = jnp.dot(jnp.concatenate([hi, lo, hi], axis=1), weight[...], preferred_element_type=F32)

    def half_turn():
        stack[...] = dotf(stack[...], inverse[...], (1, 1))

    def turn():
        stack[...] = dotf(stack[...], inverse[...], (1, 0))
        index = step_ref[...]
        lane = lax.broadcasted_iota(jnp.int32, (1, N), 1)
        latest = jnp.sum(jnp.where(index == jnp.max(index, axis=1, keepdims=True), lane, 0), axis=1, keepdims=True)
        chosen = lax.broadcasted_iota(jnp.int32, (N, N), 0) == latest
        now[...] = jnp.sum(jnp.where(chosen, stack[:N, :], 0.0), axis=0, keepdims=True) + stack[N:, :]
        states[...] = jnp.zeros((8, N), F32)
        states[0:1, :] = now[:1, :]

    def advance(i):
        now[...] = row_dot(now[...], split3(stack[:N, :]), (1, 0)) + stack[N:, :]
        states[i : i + 1, :] = now[:1, :]

    def coefficients():
        c_ref[...] = row_dot(states[...], split3(upper[...]), (1, 1))[:STEPS, :]

    def residual(*chunks):
        last = states[2:3, :]
        before = states[1:2, :]
        lane = lax.broadcasted_iota(jnp.int32, (B, B), 1)
        for chunk in chunks:
            columns = jnp.zeros((B, B), F32)
            for g in range(groups):
                at = chunk * groups + g
                s = ch_ref[at].astype(F32) + cl_ref[at].astype(F32)
                z = y_ref[at * B : (at + 1) * B, :] * last - s * before
                z = jnp.sum(z[:, :B] + z[:, B:], axis=1, keepdims=True)
                columns = jnp.where(lane == g, z, columns)
            rows = slice(chunk * groups, (chunk + 1) * groups)
            res_ref[rows, :] = columns.T[:groups, :] - STEP * f_ref[rows, :]

    def start():
        half_turn()
        turn()

    def march():
        for i in range(1, STEPS):
            advance(i)

    def first_half():
        residual(0, 1, 2, 3)
        coefficients()

    pieces = [start, march, first_half, functools.partial(residual, 4, 5, 6, 7)]

    @pl.when(step == 0)
    def _():
        factor_step(x_ref, weight, inverse, stack, upper)

    for k, piece in enumerate(pieces):

        @pl.when(step == k + 1)
        def _(piece=piece):
            basis()
            piece()


def finish(total, step_index, forcing, cand_h, cand_l, y):
    rows = y.shape[0]
    whole = pl.BlockSpec(memory_space=pltpu.VMEM)
    return pl.pallas_call(
        finish_kernel,
        grid=(rows // SPAN + 1,),
        in_specs=[whole] * 6,
        out_specs=[pl.BlockSpec((SPAN, N), lambda i: (jnp.maximum(i - 1, 0), 0)), whole, whole],
        out_shape=[
            jax.ShapeDtypeStruct((rows, N), F32),
            jax.ShapeDtypeStruct((STEPS, N), F32),
            jax.ShapeDtypeStruct((rows // B, B), F32),
        ],
        scratch_shapes=[
            pltpu.VMEM((3 * N, N), BF16),
            pltpu.VMEM((N, N), F32),
            pltpu.VMEM((N + 8, N), F32),
            pltpu.VMEM((N, N), F32),
            pltpu.VMEM((8, N), F32),
            pltpu.VMEM((8, N), F32),
        ],
        compiler_params=pltpu.CompilerParams(vmem_limit_bytes=28 << 20),
        cost_estimate=pl.CostEstimate(flops=6 * rows * N * N, bytes_accessed=4 * rows * N, transcendentals=0),
        name="finish",
    )(total, step_index.reshape(1, N), forcing, cand_h, cand_l, y)


def shards(snapshots, tangent, pattern, forcing, step_index):
    rows = snapshots.shape[0]
    blocks = rows // B
    cand_h, cand_l, gram_local = front(snapshots)
    force = forcing.reshape(blocks, B)
    y, total = image(pattern.T, tangent, force, gram_local, cand_h, cand_l)
    basis, coefficients, residual = finish(total, step_index, force, cand_h, cand_l, y)
    return basis, coefficients, residual.reshape(rows)


def solution(mesh):
    both = ("rows", "zone")
    in_specs = (P(both, None), P(both, None), P(both, None), P(both), P())
    out_specs = (P(both, None), P(), P(both))
    return jax.shard_map(shards, mesh=mesh, in_specs=in_specs, out_specs=out_specs, check_vma=False)
```

```python
import functools

import jax
import jax.numpy as jnp
from jax import lax
from jax.experimental import pallas as pl
from jax.experimental.pallas import tpu as pltpu
from jax.sharding import PartitionSpec as P

HALO = 4
STEPS = 3
STEP = 0.25
B = 128
N = 256
CHUNK = 1024
SPAN = 2048
PACK = 1344
F32 = jnp.float32
BF16 = jnp.bfloat16
HI = lax.Precision.HIGHEST
MESH = pl.DeviceIdType.MESH


def split(x):
    hi = x.astype(BF16)
    return hi, (x - hi.astype(F32)).astype(BF16)


def tdot(a, b):
    return lax.dot_general(a, b, (((0,), (0,)), ((), ())), preferred_element_type=F32)


def front_kernel(s_hbm, ch_ref, cl_ref, g_ref, sbuf, halo, load_sem, send_sem, recv_sem):
    rows = s_hbm.shape[0]
    edge = HALO * B
    chunks = rows // CHUNK
    ring, belt = lax.axis_size("rows"), lax.axis_size("zone")
    row_id, zone_id = lax.axis_index("rows"), lax.axis_index("zone")
    loads = []
    for i in range(chunks):
        part = pl.ds(i * CHUNK, CHUNK)
        loads.append(pltpu.make_async_copy(s_hbm.at[part], sbuf.at[part], load_sem.at[i]))
        loads[-1].start()
    peers = (
        ((row_id + 1) % ring, zone_id),
        ((row_id + ring - 1) % ring, zone_id),
        (row_id, (zone_id + 1) % belt),
        (row_id, (zone_id + belt - 1) % belt),
    )
    barrier = pltpu.get_barrier_semaphore()
    for peer in peers:
        pl.semaphore_signal(barrier, inc=1, device_id=peer, device_id_type=MESH)
    pl.semaphore_wait(barrier, 4)
    copies = []
    for i, peer in enumerate(peers):
        start = rows - edge if i % 2 == 0 else 0
        copies.append(
            pltpu.make_async_remote_copy(
                src_ref=s_hbm.at[pl.ds(start, edge)], dst_ref=halo.at[i],
                send_sem=send_sem.at[i], recv_sem=recv_sem.at[i], device_id=peer, device_id_type=MESH,
            )
        )
        copies[-1].start()
    total = jnp.zeros((2 * N, N), F32)
    for i in range(chunks):
        loads[i].wait()
        part = pl.ds(i * CHUNK, CHUNK)
        hi, lo = split(sbuf[part, :])
        spot = pl.ds(i * CHUNK // B, CHUNK // B)
        ch_ref[spot] = hi.reshape(CHUNK // B, B, N)
        cl_ref[spot] = lo.reshape(CHUNK // B, B, N)
        total += tdot(jnp.concatenate([hi, lo], axis=1), hi)
    half = total[:N] * 0.5 + total[N:]
    g_ref[...] = half + half.T
    there = (True, True, zone_id > 0, zone_id < belt - 1)
    for i in (2, 3, 0, 1):
        copies[i].wait_recv()
        value = halo[i]
        if i >= 2:
            value = jnp.where(there[i], value, 0.0)
        hi, lo = split(value)
        spot = pl.ds(rows // B + i * HALO, HALO)
        ch_ref[spot] = hi.reshape(HALO, B, N)
        cl_ref[spot] = lo.reshape(HALO, B, N)
    for copy in copies:
        copy.wait_send()


def front(snapshots):
    rows = snapshots.shape[0]
    edge = HALO * B
    return pl.pallas_call(
        front_kernel,
        in_specs=[pl.BlockSpec(memory_space=pl.ANY)],
        out_specs=[pl.BlockSpec(memory_space=pltpu.VMEM)] * 3,
        out_shape=[
            jax.ShapeDtypeStruct((rows // B + 4 * HALO, B, N), BF16),
            jax.ShapeDtypeStruct((rows // B + 4 * HALO, B, N), BF16),
            jax.ShapeDtypeStruct((N, N), F32),
        ],
        scratch_shapes=[
            pltpu.VMEM((rows, N), F32),
            pltpu.VMEM((4, edge, N), F32),
            pltpu.SemaphoreType.DMA((rows // CHUNK,)),
            pltpu.SemaphoreType.DMA((4,)),
            pltpu.SemaphoreType.DMA((4,)),
        ],
        compiler_params=pltpu.CompilerParams(collective_id=1, has_side_effects=True, vmem_limit_bytes=38 << 20),
        cost_estimate=pl.CostEstimate(flops=2 * rows * N * N, bytes_accessed=8 * rows * N, transcendentals=0),
        name="front",
    )(snapshots)


PARTS = 3
PART = PACK // PARTS
STAGE_SLOTS = (1, 3, 3, 3, 3, 1)
STAGE_BASE = tuple(PARTS * sum(STAGE_SLOTS[:i]) for i in range(6))


def reach():
    rows_id = lax.axis_index("rows")
    zone_id = lax.axis_index("zone")
    core = zone_id % 2
    place = {"x": zone_id // 2, "y": rows_id % 4, "z": rows_id // 4}
    def device(axis, shift):
        at = dict(place)
        if axis == "core":
            return (rows_id, at["x"] * 2 + (1 - core))
        at[axis] = (at[axis] + shift) % 4
        return (at["z"] * 4 + at["y"], at["x"] * 2 + core)

    return core, place, device


def greet():
    _, _, device = reach()
    barrier = pltpu.get_barrier_semaphore()
    for axis, shift in [("core", 1)] + [(a, s) for a in "xyz" for s in (1, 2, 3)]:
        pl.semaphore_signal(barrier, inc=1, device_id=device(axis, shift), device_id_type=MESH)


def reduce_all(x_ref, o_ref, acc, got0, got1, got2, got3, send_sem, recv_sem):
    core, place, device = reach()
    pl.semaphore_wait(pltpu.get_barrier_semaphore(), 10)
    live = {}

    def send(stage, part, slot, src, dst, axis, shift):
        k = STAGE_BASE[stage] + part * STAGE_SLOTS[stage] + slot
        copy = pltpu.make_async_remote_copy(
            src_ref=src, dst_ref=dst, send_sem=send_sem.at[k], recv_sem=recv_sem.at[k],
            device_id=device(axis, shift), device_id_type=MESH,
        )
        copy.start()
        live[stage, part, slot] = copy

    def arrive(stage, part):
        for slot in range(STAGE_SLOTS[stage]):
            live[stage, part, slot].wait_recv()

    orders = (("x", "y", "z"), ("y", "z", "x"), ("z", "x", "y"))
    half = PART // 2
    quarter = half // 4
    mine = core * half
    for p in range(PARTS):
        send(0, p, 0, x_ref.at[pl.ds(p * PART + (1 - core) * half, half)], got0.at[p], "core", 1)
    for p, (a, b, c) in enumerate(orders):
        arrive(0, p)
        acc[p] = x_ref[pl.ds(p * PART + mine, half), :] + got0[p]
        for o in (2, 1, 3):
            there = (place[a] + o) % 4
            send(1, p, o - 1, acc.at[p, pl.ds(there * quarter, quarter)], got1.at[p, o - 1], a, o)
    for p, (a, b, c) in enumerate(orders):
        arrive(1, p)
        slot = got2.at[p, place[b]]
        slot[...] = acc[p, pl.ds(place[a] * quarter, quarter), :] + got1[p, 0] + got1[p, 1] + got1[p, 2]
        for o in (2, 1, 3):
            send(2, p, o - 1, slot, slot, b, o)
    for p, (a, b, c) in enumerate(orders):
        arrive(2, p)
        slot = got3.at[p, place[c]]
        slot[...] = got2[p, 0] + got2[p, 1] + got2[p, 2] + got2[p, 3]
        for o in (2, 1, 3):
            send(3, p, o - 1, slot, slot, c, o)
    for p, (a, b, c) in enumerate(orders):
        arrive(3, p)
        spot = o_ref.at[pl.ds(p * PART + mine + place[a] * quarter, quarter)]
        spot[...] = got3[p, 0] + got3[p, 1] + got3[p, 2] + got3[p, 3]
        for o in (2, 1, 3):
            send(4, p, o - 1, spot, spot, a, o)
    for p in range(PARTS):
        arrive(4, p)
        spot = o_ref.at[pl.ds(p * PART + mine, half)]
        send(5, p, 0, spot, spot, "core", 1)
    for p in range(PARTS):
        arrive(5, p)
    for copy in live.values():
        copy.wait_send()


def decode(code, blocks):
    source = code // blocks
    block = code % blocks
    tail = jnp.where((source == 1) | (source == 3), blocks - HALO, 0)
    return jnp.where(source == 0, block, blocks + HALO * (source - 1) + block - tail)


def image_kernel(
    code_ref, t_ref, f_ref, g_ref, cand_h, cand_l, y_ref, total_ref,
    ybuf_h, ybuf_l, acc, load_acc, pack_ref, *exchange,
):
    step = pl.program_id(0)

    @pl.when(step == 0)
    def _():
        greet()
        acc[...] = jnp.zeros_like(acc)
        load_acc[...] = jnp.zeros_like(load_acc)

    groups = CHUNK // B
    force = f_ref[...].T
    total = jnp.zeros((8, N), F32)
    for g in range(groups):
        picks = [decode(code_ref[e, step * groups + g], cand_h.shape[0] - 4 * HALO) for e in range(4)]
        tiles = t_ref[g * B : (g + 1) * B, :]
        image = jnp.dot(tiles, jnp.concatenate([cand_h[p] for p in picks], axis=0), preferred_element_type=F32)
        image += jnp.dot(tiles, jnp.concatenate([cand_l[p] for p in picks], axis=0), preferred_element_type=F32)
        own = pl.ds(pl.multiple_of(step * CHUNK + g * B, B), B)
        y = cand_h[step * groups + g].astype(F32) + cand_l[step * groups + g].astype(F32) + STEP * image
        y_ref[own, :] = y
        hi, lo = split(y)
        ybuf_h[g * B : (g + 1) * B, :] = hi
        ybuf_l[g * B : (g + 1) * B, :] = lo
        total += jnp.sum((y * force[:, g : g + 1]).reshape(B // 8, 8, N), axis=0)
    load_acc[...] += total
    here = pl.ds(step * groups, groups)
    yh = ybuf_h[...]
    yl = ybuf_l[...]
    one = tdot(jnp.concatenate([yh, yl], axis=1), cand_h[here].reshape(CHUNK, N))
    acc[0] += one[:N] + one[N:]
    two = tdot(jnp.concatenate([yh, yl, cand_l[here].reshape(CHUNK, N)], axis=1), yh)
    acc[1] += two[:N] * 0.5 + two[N : 2 * N]
    acc[2] += two[2 * N :]

    @pl.when(step == pl.num_programs(0) - 1)
    def _():
        normal = acc[1] + acc[1].T
        project = acc[0] + acc[2].T
        gram_matrix = g_ref[...]
        blocks = []
        for matrix in (gram_matrix, normal):
            blocks += [matrix[:B, :B], matrix[:B, B:], matrix[B:, B:]]
        blocks += [project[:B, :B], project[:B, B:], project[B:, :B], project[B:, B:]]
        for i, block in enumerate(blocks):
            pack_ref[i * B : (i + 1) * B, :] = block
        load = jnp.sum(load_acc[...], axis=0, keepdims=True)
        pack_ref[10 * B :, :] = jnp.zeros((PACK - 10 * B, B), F32)
        pack_ref[10 * B : 10 * B + 1, :] = load[:, :B]
        pack_ref[10 * B + 1 : 10 * B + 2, :] = load[:, B:]
        reduce_all(pack_ref, *exchange)
        total_ref[...] = exchange[0][...]


def image(codes, tangent, forcing, gram_local, cand_h, cand_l):
    rows = tangent.shape[0]
    half = PART // 2
    count = PARTS * sum(STAGE_SLOTS)
    return pl.pallas_call(
        image_kernel,
        grid_spec=pltpu.PrefetchScalarGridSpec(
            num_scalar_prefetch=1,
            grid=(rows // CHUNK,),
            in_specs=[
                pl.BlockSpec((CHUNK, 4 * B), lambda i, *_: (i, 0)),
                pl.BlockSpec((CHUNK // B, B), lambda i, *_: (i, 0)),
                pl.BlockSpec(memory_space=pltpu.VMEM),
                pl.BlockSpec(memory_space=pltpu.VMEM),
                pl.BlockSpec(memory_space=pltpu.VMEM),
            ],
            out_specs=[
                pl.BlockSpec(memory_space=pltpu.VMEM),
                pl.BlockSpec(memory_space=pltpu.VMEM),
            ],
            scratch_shapes=[
                pltpu.VMEM((CHUNK, N), BF16),
                pltpu.VMEM((CHUNK, N), BF16),
                pltpu.VMEM((3, N, N), F32),
                pltpu.VMEM((8, N), F32),
                pltpu.VMEM((PACK, B), F32),
                pltpu.VMEM((PACK, B), F32),
                pltpu.VMEM((PARTS, half, B), F32),
                pltpu.VMEM((PARTS, half, B), F32),
                pltpu.VMEM((PARTS, 3, half // 4, B), F32),
                pltpu.VMEM((PARTS, 4, half // 4, B), F32),
                pltpu.VMEM((PARTS, 4, half // 4, B), F32),
                pltpu.SemaphoreType.DMA((count,)),
                pltpu.SemaphoreType.DMA((count,)),
            ],
        ),
        out_shape=[
            jax.ShapeDtypeStruct((rows, N), F32),
            jax.ShapeDtypeStruct((PACK, B), F32),
        ],
        compiler_params=pltpu.CompilerParams(collective_id=0, has_side_effects=True, vmem_limit_bytes=28 << 20),
        cost_estimate=pl.CostEstimate(flops=20 * rows * N * N, bytes_accessed=8 * rows * N, transcendentals=0),
        name="image",
    )(codes, tangent, forcing, gram_local, cand_h, cand_l)


def split3f(x):
    hi = x.astype(BF16).astype(F32)
    mid = (x - hi).astype(BF16).astype(F32)
    return hi, mid, (x - hi - mid)


def factor_blocks(matrices):
    tiles = [[m[8 * t : 8 * t + 8, :] for t in range(16)] for m in matrices]
    lane = lax.broadcasted_iota(jnp.int32, (8, B), 1)
    sub = lax.broadcasted_iota(jnp.int32, (8, B), 0)
    inverse = [[(lane == sub + 8 * t).astype(F32) for t in range(16)] for _ in matrices]
    for p in range(16):
        for a, e in zip(tiles, inverse):
            spread = lambda t: [jnp.broadcast_to(a[t][:, 8 * p + c : 8 * p + c + 1], (8, B)) for c in range(8)]
            column = spread(p)
            pivot, link = [], {}
            for k in range(8):
                pivot.append(lax.rsqrt(column[k][k : k + 1, :]))
                column[k] = column[k] * pivot[k]
                for c in range(k + 1, 8):
                    link[k, c] = column[k][c : c + 1, :]
                    column[c] = column[c] - column[k] * link[k, c]
            rows, erows = [], []
            own, eown = a[p], e[p]
            for k in range(8):
                rows.append(own[k : k + 1, :] * pivot[k])
                erows.append(eown[k : k + 1, :] * pivot[k])
                own = own - column[k] * rows[k]
                eown = eown - column[k] * erows[k]
            if p + 1 < 16:
                t = p + 1
                column = spread(t)
                for k in range(8):
                    column[k] = column[k] * pivot[k]
                    for c in range(k + 1, 8):
                        column[c] = column[c] - column[k] * link[k, c]
                    a[t] = a[t] - column[k] * rows[k]
                    e[t] = e[t] - column[k] * erows[k]
            a[p] = jnp.concatenate(rows, axis=0)
            e[p] = jnp.concatenate(erows, axis=0)
            if p + 2 < 16:
                ah, am, al = split3f(a[p])
                eh, em, el = split3f(e[p])
                lhs = jnp.concatenate([ah, ah, am, ah, al, am], axis=0).astype(BF16)
                rhs = jnp.concatenate(
                    [jnp.concatenate([ah, am, ah, al, ah, am], axis=0), jnp.concatenate([eh, em, eh, el, eh, em], axis=0)], axis=1
                ).astype(BF16)
                update = tdot(lhs, rhs)
                for t in range(p + 2, 16):
                    a[t] = a[t] - update[8 * t : 8 * t + 8, :B]
                    e[t] = e[t] - update[8 * t : 8 * t + 8, B:]
    upper = [
        jnp.concatenate([jnp.where(lane >= sub + 8 * t, a[t], 0.0) for t in range(16)], axis=0) for a in tiles
    ]
    return upper, [jnp.concatenate(e, axis=0) for e in inverse]


def dotf(a, b, dims):
    return lax.dot_general(a, b, ((dims[:1], dims[1:]), ((), ())), precision=HI, preferred_element_type=F32)


def split3(x):
    hi = x.astype(BF16)
    rest = x - hi.astype(F32)
    mid = rest.astype(BF16)
    return hi, mid, (rest - mid.astype(F32)).astype(BF16)


def row_dot(a, b, dims):
    hi, mid, low = split3(a)
    dot = lambda x, y: lax.dot_general(x, y, ((dims[:1], dims[1:]), ((), ())), preferred_element_type=F32)
    rows = [t.astype(F32) for t in (hi, mid, low)]
    one = dot(jnp.concatenate(rows, axis=0).astype(BF16), b[0])
    two = dot(jnp.concatenate(rows[:2], axis=0).astype(BF16), b[1])
    three = dot(hi, b[2])
    return (one[16:] + two[8:16] + three) + (one[8:16] + two[:8]) + one[:8]


def factor_step(x_ref, weight, inverse, stack, upper):
    scale = 1.0 / (8192 * 128)
    block = lambda i: x_ref[i * B : (i + 1) * B, :] * scale
    g11, g12, g22, n11, n12, n22 = (block(i) for i in range(6))
    (u_g, u_n), (e_g, e_n) = factor_blocks([g11, n11])
    u12_g = dotf(e_g, g12, (1, 0))
    u12_n = dotf(e_n, n12, (1, 0))
    s_g = g22 - dotf(u12_g, u12_g, (0, 0))
    s_n = n22 - dotf(u12_n, u12_n, (0, 0))
    (v_g, v_n), (h_g, h_n) = factor_blocks([s_g, s_n])
    low_g = -dotf(h_g, dotf(u12_g, e_g, (0, 0)), (1, 0))
    low_n = -dotf(h_n, dotf(u12_n, e_n, (0, 0)), (1, 0))
    zero = jnp.zeros((B, B), F32)
    hi, lo = split(
        jnp.concatenate(
            [jnp.concatenate([e_g.T, low_g.T], axis=1), jnp.concatenate([zero, h_g.T], axis=1)], axis=0
        )
    )
    weight[:N, :] = hi
    weight[N : 2 * N, :] = hi
    weight[2 * N :, :] = lo
    inverse[...] = jnp.concatenate(
        [jnp.concatenate([e_n, zero], axis=1), jnp.concatenate([low_n, h_n], axis=1)], axis=0
    )
    upper[...] = jnp.concatenate(
        [jnp.concatenate([u_g, u12_g], axis=1), jnp.concatenate([zero, v_g], axis=1)], axis=0
    )
    project = jnp.concatenate(
        [jnp.concatenate([block(6), block(7)], axis=1), jnp.concatenate([block(8), block(9)], axis=1)], axis=0
    )
    load = jnp.concatenate([x_ref[10 * B : 10 * B + 1, :], x_ref[10 * B + 1 : 10 * B + 2, :]], axis=1)
    stack[:N, :] = project.T
    stack[N:, :] = jnp.broadcast_to(load * (scale * STEP), (8, N))


def finish_kernel(
    x_ref, step_ref, f_ref, ch_ref, cl_ref, y_ref, basis_ref, c_ref, res_ref,
    weight, inverse, stack, upper, now, states,
):
    step = pl.program_id(0)
    groups = CHUNK // B

    def basis():
        here = pl.ds((step - 1) * (SPAN // B), SPAN // B)
        hi = ch_ref[here].reshape(SPAN, N)
        lo = cl_ref[here].reshape(SPAN, N)
        basis_ref[...] = jnp.dot(jnp.concatenate([hi, lo, hi], axis=1), weight[...], preferred_element_type=F32)

    def half_turn():
        stack[...] = dotf(stack[...], inverse[...], (1, 1))

    def turn():
        stack[...] = dotf(stack[...], inverse[...], (1, 0))
        index = step_ref[...]
        lane = lax.broadcasted_iota(jnp.int32, (1, N), 1)
        latest = jnp.sum(jnp.where(index == jnp.max(index, axis=1, keepdims=True), lane, 0), axis=1, keepdims=True)
        chosen = lax.broadcasted_iota(jnp.int32, (N, N), 0) == latest
        now[...] = jnp.sum(jnp.where(chosen, stack[:N, :], 0.0), axis=0, keepdims=True) + stack[N:, :]
        states[...] = jnp.zeros((8, N), F32)
        states[0:1, :] = now[:1, :]

    def advance(i):
        now[...] = row_dot(now[...], split3(stack[:N, :]), (1, 0)) + stack[N:, :]
        states[i : i + 1, :] = now[:1, :]

    def coefficients():
        c_ref[...] = row_dot(states[...], split3(upper[...]), (1, 1))[:STEPS, :]

    def residual(*chunks):
        last = states[2:3, :]
        before = states[1:2, :]
        lane = lax.broadcasted_iota(jnp.int32, (B, B), 1)
        for chunk in chunks:
            columns = jnp.zeros((B, B), F32)
            for g in range(groups):
                at = chunk * groups + g
                s = ch_ref[at].astype(F32) + cl_ref[at].astype(F32)
                z = y_ref[at * B : (at + 1) * B, :] * last - s * before
                z = jnp.sum(z[:, :B] + z[:, B:], axis=1, keepdims=True)
                columns = jnp.where(lane == g, z, columns)
            rows = slice(chunk * groups, (chunk + 1) * groups)
            res_ref[rows, :] = columns.T[:groups, :] - STEP * f_ref[rows, :]

    def start():
        half_turn()
        turn()

    def march():
        for i in range(1, STEPS):
            advance(i)

    def first_half():
        residual(0, 1, 2, 3)
        coefficients()

    pieces = [start, march, first_half, functools.partial(residual, 4, 5, 6, 7)]

    @pl.when(step == 0)
    def _():
        factor_step(x_ref, weight, inverse, stack, upper)

    for k, piece in enumerate(pieces):

        @pl.when(step == k + 1)
        def _(piece=piece):
            basis()
            piece()


def finish(total, step_index, forcing, cand_h, cand_l, y):
    rows = y.shape[0]
    whole = pl.BlockSpec(memory_space=pltpu.VMEM)
    return pl.pallas_call(
        finish_kernel,
        grid=(rows // SPAN + 1,),
        in_specs=[whole] * 6,
        out_specs=[pl.BlockSpec((SPAN, N), lambda i: (jnp.maximum(i - 1, 0), 0)), whole, whole],
        out_shape=[
            jax.ShapeDtypeStruct((rows, N), F32),
            jax.ShapeDtypeStruct((STEPS, N), F32),
            jax.ShapeDtypeStruct((rows // B, B), F32),
        ],
        scratch_shapes=[
            pltpu.VMEM((3 * N, N), BF16),
            pltpu.VMEM((N, N), F32),
            pltpu.VMEM((N + 8, N), F32),
            pltpu.VMEM((N, N), F32),
            pltpu.VMEM((8, N), F32),
            pltpu.VMEM((8, N), F32),
        ],
        compiler_params=pltpu.CompilerParams(vmem_limit_bytes=28 << 20),
        cost_estimate=pl.CostEstimate(flops=6 * rows * N * N, bytes_accessed=4 * rows * N, transcendentals=0),
        name="finish",
    )(total, step_index.reshape(1, N), forcing, cand_h, cand_l, y)


def shards(snapshots, tangent, pattern, forcing, step_index):
    rows = snapshots.shape[0]
    blocks = rows // B
    cand_h, cand_l, gram_local = front(snapshots)
    force = forcing.reshape(blocks, B)
    y, total = image(pattern.T, tangent, force, gram_local, cand_h, cand_l)
    basis, coefficients, residual = finish(total, step_index, force, cand_h, cand_l, y)
    return basis, coefficients, residual.reshape(rows)


def solution(mesh):
    both = ("rows", "zone")
    in_specs = (P(both, None), P(both, None), P(both, None), P(both), P())
    out_specs = (P(both, None), P(), P(both))
    return jax.shard_map(shards, mesh=mesh, in_specs=in_specs, out_specs=out_specs, check_vma=False)
```
